256 devices in a mesh: src: 16 (over x, y), dst: 16 (over z, core).
Axes of the slice: x: 4, y: 4, z: 8, core: 2. Of those that a mesh axis runs over, the one named last changes fastest.
Arguments:
- density0: float32 [16, 131072], P(None, ('src', 'dst')), may hold values from 0.2 to 5
- logits: float32 [2, 16, 131072], P(None, None, ('src', 'dst')), may hold values from -6 to 6
- value_final: float32 [16, 131072], P(None, ('src', 'dst')), may hold values from -6 to 6
- base_reward: float32 [2, 16, 131072], P(None, None, ('src', 'dst')), may hold values from -6 to 6
- crowd: float32 [16], replicated, may hold values from 0.2 to 2
- tiles: bfloat16 [16, 16, 2, 8, 256, 256], P('src', 'dst'), may hold values from 0 to 0.75
- tile_src: int32 [16, 16, 2, 8], P('src', 'dst'), may hold values from 0 to 31
- tile_dst: int32 [16, 16, 2, 8], P('src', 'dst'), may hold values from 0 to 31
- tile_count: int32 [16, 16, 2], P('src', 'dst'), may hold values from 2 to 8, as said below
Outputs:
- new_logits: float32 [2, 16, 131072], P(None, None, ('src', 'dst'))
- value_start: float32 [16, 131072], P(None, ('src', 'dst'))
- density_final: float32 [16, 131072], P(None, ('src', 'dst'))
The draws below stay inside these ranges and needn't reach their ends.
Inputs may be any that keep to these rules, and one draw needn't show every extreme that they name: `tile_count`: slots at or past the count are ignored. In every draw some device holds 8 live slots for some action.
All inputs are finite; a program needn't handle non-finite values.
Results may differ from the reference program's by a relative error of at most 0.0011.
Values may be sent and summed in bfloat16 or wider, within the bound.
No kernel may reach another device: no remote copies, remote signals or barrier semaphores. Data moves between devices by JAX's collectives and lax.ppermute only.
A program may use at most 64 MiB of HBM per device.

```python
import math
import jax
import jax.numpy as jnp
from jax import lax

P_SIZE = 16
A = 2
B = 256
BPZ = 2
TCAP = 8
H = 4
BS_SRC = 32
BS_DST = 32
NSTATES = 131072
N_SRC = 16
N_DST = 16


def draw_tile_count(key, part):
    first, second, third = jax.random.split(jax.random.fold_in(key, 17), 3)
    shape = (N_SRC, N_DST, A)
    base = jax.random.randint(first, shape, TCAP // 4, TCAP // 2 + 1)
    hubs = jax.random.randint(second, shape, 0, 8) == 0
    forced = jax.random.randint(third, (), 0, N_SRC * N_DST * A)
    flat_index = jnp.arange(N_SRC * N_DST * A, dtype=jnp.int32).reshape(shape)
    chosen = jnp.logical_or(hubs, flat_index == forced)
    return jnp.where(chosen, TCAP, base).astype(jnp.int32)


def draw_tiles(key, part):
    keys = jax.random.split(jax.random.fold_in(key, 29), 4)
    lead = (N_SRC, N_DST, A, TCAP)
    offset = jax.random.randint(keys[0], lead + (1, 1), 0, B)
    jitter = jax.random.randint(keys[1], lead + (B, 1), -2, 3)
    band = jax.random.randint(keys[2], lead + (B, 1), 8, 17)
    rows = jnp.arange(B, dtype=jnp.int32)[:, None]
    cols = jnp.arange(B, dtype=jnp.int32)[None, :]
    first_col = rows + offset + jitter - band // 2
    inside = jnp.mod(cols - first_col, B) < band
    factor_scale = 2.0 * BPZ / (TCAP * 37.0)
    factor = jnp.exp(1.5 * jax.random.truncated_normal(keys[3], -2.5, 2.5, lead + (B, B), jnp.float32))
    values = factor * factor_scale
    return jnp.where(inside, values, 0.0).astype(jnp.bfloat16)


def touch_ends(values, stream_key, smallest, top_value):
    shape = values.shape
    index_at = [jax.random.randint(jax.random.fold_in(stream_key, axis), (), 0, shape[axis]) for axis in range(len(shape))]
    values = values.at[tuple(index_at)].set(smallest)
    longest = shape.index(max(shape))
    index_at[longest] = (index_at[longest] + 1) % shape[longest]
    return values.at[tuple(index_at)].set(top_value)


def steps_of(own_key, dims, pieces, low, high):
    factor_of, own = 1.0, jax.random.fold_in(own_key, 6)
    for dim, blocks in pieces:
        heights = jnp.exp(jax.random.uniform(jax.random.fold_in(own, dim), (blocks,), jnp.float32, low / len(pieces), high / len(pieces)))
        factor_of = factor_of * jnp.repeat(heights, dims[dim] // blocks).reshape([-1 if axis == dim else 1 for axis in range(len(dims))])
    return factor_of


def normal_values(rng, dims, scale, bound, cuts=(), kind=jnp.bfloat16):
    values = jax.random.normal(rng, dims, jnp.float32) * scale
    if len(cuts) > 0:
        values = steps_of(rng, dims, cuts, -0.22, 0.18) * values
    return jnp.clip(values, min=-bound, max=bound).astype(kind)


def setup_inputs(seed: int = 0) -> dict:
    streams_of = jax.random.split(jax.random.key(seed), 10)
    density0 = jnp.clip(jnp.exp(math.log(5.0) - 3.218876 * jax.random.uniform(streams_of[0], (P_SIZE, NSTATES), jnp.float32) ** steps_of(streams_of[0], (P_SIZE, NSTATES), ((1, 256),), -0.2, 0.2)), 0.2, 5.0)
    logits = normal_values(streams_of[1], (A, P_SIZE, NSTATES), 1.0, 6.0, ((2, 256),), jnp.float32)
    value_final = normal_values(streams_of[2], (P_SIZE, NSTATES), 1.0, 6.0, ((1, 256),), jnp.float32)
    base_reward = normal_values(streams_of[3], (A, P_SIZE, NSTATES), 1.0, 6.0, ((2, 256),), jnp.float32)
    crowd = jnp.clip(jnp.exp(jax.random.uniform(streams_of[4], (P_SIZE,), jnp.float32, math.log(0.2), math.log(2.0))), 0.2, 2.0)
    tiles = draw_tiles(jax.random.fold_in(streams_of[9], 71), 0)
    tile_src = touch_ends(jax.random.randint(streams_of[6], (N_SRC, N_DST, A, TCAP), 0, BS_SRC), jax.random.fold_in(streams_of[6], 1), 0, BS_SRC - 1).astype(jnp.int32)
    tile_dst = touch_ends(jax.random.randint(streams_of[7], (N_SRC, N_DST, A, TCAP), 0, BS_DST), jax.random.fold_in(streams_of[7], 1), 0, BS_DST - 1).astype(jnp.int32)
    tile_count = draw_tile_count(jax.random.fold_in(streams_of[9], 71), 0)
    return dict(density0=density0, logits=logits, value_final=value_final, base_reward=base_reward, crowd=crowd, tiles=tiles, tile_src=tile_src, tile_dst=tile_dst, tile_count=tile_count)


discount = 0.9
step_size = 1.0


def policy_of(logits):
    margin = logits[0] - logits[1]
    return jnp.stack([jax.nn.sigmoid(margin), jax.nn.sigmoid(-margin)])


def reward_of(base_reward, crowd, density):
    crowding = jnp.log1p(jnp.mean(density, axis=0))
    return base_reward - crowd[None, :, None] * crowding[None, None, :]


def take_rows(block_set, row_index):
    return jnp.take(block_set, row_index, axis=1)


def add_rows(target, row_index, update):
    return target.at[:, row_index, :].add(update)


def reference(density0, logits, value_final, base_reward, crowd, tiles, tile_src, tile_dst, tile_count):
    device_total = N_SRC * N_DST
    blocks_all = NSTATES // B
    src_index = jnp.arange(N_SRC, dtype=jnp.int32)[:, None, None, None]
    dst_index = jnp.arange(N_DST, dtype=jnp.int32)[None, :, None, None]
    src_global = (src_index * BS_SRC + tile_src).astype(jnp.int32)
    dst_global = (((tile_dst // BPZ) * N_DST + dst_index) * BPZ + tile_dst % BPZ).astype(jnp.int32)
    slot_index = jnp.arange(TCAP, dtype=jnp.int32)[None, None, None, :]
    live = (slot_index < tile_count[..., None]).astype(jnp.float32)
    tile_flat = tiles.reshape(device_total, A, TCAP, B, B)
    src_flat = src_global.reshape(device_total, A, TCAP)
    dst_flat = dst_global.reshape(device_total, A, TCAP)
    live_flat = live.reshape(device_total, A, TCAP)
    policy_now = policy_of(logits)

    def forward_raw(weighted):
        blocks = weighted.reshape(A, P_SIZE, blocks_all, B)

        def visit(accum, item):
            tile_block, src_rows, dst_rows, active = item
            picked = jax.vmap(take_rows)(blocks, src_rows)
            product = jnp.einsum('apki,akij->apkj', picked.astype(jnp.float32), tile_block.astype(jnp.float32), precision=lax.Precision.HIGHEST)
            product = product * active[:, None, :, None]
            flat = jnp.transpose(product, (1, 0, 2, 3)).reshape(P_SIZE, A * TCAP, B)
            return accum.at[:, dst_rows.reshape(-1), :].add(flat), None

        start = jnp.zeros((P_SIZE, blocks_all, B), jnp.float32)
        result, _ = lax.scan(visit, start, (tile_flat, src_flat, dst_flat, live_flat))
        return result.reshape(P_SIZE, NSTATES)

    def backward_raw(value_half):
        blocks = value_half.reshape(P_SIZE, blocks_all, B)

        def pick_columns(dst_action):
            return jnp.take(blocks, dst_action, axis=1)

        def visit(accum, item):
            tile_block, src_rows, dst_rows, active = item
            picked = jax.vmap(pick_columns)(dst_rows)
            product = jnp.einsum('akij,apkj->apki', tile_block.astype(jnp.float32), picked.astype(jnp.float32), precision=lax.Precision.HIGHEST)
            product = product * active[:, None, :, None]
            return jax.vmap(add_rows)(accum, src_rows, product), None

        start = jnp.zeros((A, P_SIZE, blocks_all, B), jnp.float32)
        result, _ = lax.scan(visit, start, (tile_flat, src_flat, dst_flat, live_flat))
        return result.reshape(A, P_SIZE, NSTATES)

    densities = [density0]
    for moment in range(H):
        weighted = (policy_now * densities[-1][None]).astype(jnp.bfloat16)
        arrived = forward_raw(weighted)
        mass = jnp.sum(arrived, axis=1)
        densities.append(arrived * (NSTATES / mass)[:, None])

    value_next = value_final
    action_value = base_reward
    for moment in reversed(range(H)):
        returned = backward_raw(value_next.astype(jnp.bfloat16))
        action_value = reward_of(base_reward, crowd, densities[moment]) + discount * returned
        value_next = jnp.sum(policy_now * action_value, axis=0)
    new_logits = logits + step_size * action_value
    return (new_logits, value_next, densities[-1])
```

```python
import jax
import jax.numpy as jnp
from jax import lax
from jax.experimental import pallas as pl
from jax.experimental.pallas import tpu as pltpu
from jax.sharding import PartitionSpec as P


P_SIZE = 16
A = 2
B = 256
BPZ = 2
TCAP = 8
H = 4

HP = P_SIZE // 2
ZB = 2 * BPZ

discount = 0.9
step_size = 1.0

F32 = jnp.float32
BF16 = jnp.bfloat16


def sigmoid(v):
    return 1.0 / (1.0 + jnp.exp(-v))


def split_parts(x):
    hi = x.astype(BF16)
    lo = (x - hi.astype(F32)).astype(BF16)
    return hi, lo


def wide_parts(col):
    hi, lo = split_parts(jnp.broadcast_to(col, (HP, B // 2)))
    return jnp.concatenate([hi, lo], axis=1)


def narrow_parts(block):
    return block[:, 0:1] + block[:, B // 2 : B // 2 + 1]


def call(kernel, outs, n_smem, scratch=()):
    def run(*args):
        specs = [pl.BlockSpec(memory_space=pltpu.SMEM)] * n_smem
        specs += [pl.BlockSpec(memory_space=pltpu.VMEM)] * (len(args) - n_smem)
        return pl.pallas_call(
            kernel,
            out_shape=[jax.ShapeDtypeStruct(s, d) for s, d in outs],
            in_specs=specs,
            out_specs=[pl.BlockSpec(memory_space=pltpu.VMEM)] * len(outs),
            scratch_shapes=list(scratch),
            compiler_params=pltpu.CompilerParams(vmem_limit_bytes=12 << 20),
        )(*args)

    return run


def slots(core, idx_refs, tile_refs):
    for which in range(2):
        origin = core if which == 0 else 1 - core
        idx = idx_refs[which]
        for a in range(A):
            count = idx[2 * A * TCAP + a]
            for k in range(TCAP):
                row = idx[a * TCAP + k]
                dst = idx[A * TCAP + a * TCAP + k]
                col = (dst // BPZ) * ZB + origin * BPZ + dst % BPZ
                live = (k < count).astype(F32)
                yield a, row, col, live, tile_refs[which], a * TCAP + k


def forward(core, idx_refs, tile_refs, pi_ref, dens_of, acc):
    acc[...] = jnp.zeros_like(acc)
    for a, row, col, live, tiles, k in slots(core, idx_refs, tile_refs):
        w = (pi_ref[a, row] * (dens_of(row).astype(F32) * live)).astype(BF16)
        acc[col] += jnp.dot(w, tiles[k], preferred_element_type=F32)


def backward(core, idx_refs, tile_refs, v_of, visit, ones=False):
    for a, row, col, live, tiles, k in slots(core, idx_refs, tile_refs):
        v = v_of(col)
        if ones:
            v = jnp.concatenate([v, jnp.ones((HP, B), BF16)], axis=0)
        r = lax.dot_general(v, tiles[k], (((1,), (1,)), ((), ())), preferred_element_type=F32)
        visit(a, row, r * live)


PARTS = {2: 1, 3: 1, 4: 1, 6: 2, 8: 1, 9: 2, 10: 1, 12: 2}

DENS = {3: 1, 5: 1, 8: 2}


def put_density(ref, at, b, x, parts):
    if parts == 1:
        put_all(ref, at + b, x.astype(BF16))
    else:
        hi, lo = split_parts(x)
        put_all(ref, at + 2 * b, hi)
        put_all(ref, at + 2 * b + 1, lo)


def density_at(ref, at, parts):
    def get(row):
        z, b = row // ZB, at + parts * (row % ZB)
        if parts == 1:
            return ref[z, b].astype(F32)
        return ref[z, b].astype(F32) + ref[z, b + 1].astype(F32)

    return get


def put_sums(ref, peer, at, blocks, parts):
    for b, x in enumerate(blocks):
        if parts == 1:
            ref[peer, at + b] = x.astype(BF16)
        else:
            hi, lo = split_parts(x)
            ref[peer, at + 2 * b] = hi
            ref[peer, at + 2 * b + 1] = lo


def get_sum(ref, at, b, parts):
    total = jnp.sum(ref[:, at + parts * b].astype(F32), axis=0)
    if parts == 2:
        total += jnp.sum(ref[:, at + 2 * b + 1].astype(F32), axis=0)
    return total


def put_all(ref, at, block):
    for peer in range(ref.shape[0]):
        ref[peer, at] = block


def k_start(density, logits, base, value, core, send, keep):
    margin = logits[0] - logits[1]
    pi0, pi1 = sigmoid(margin), sigmoid(-margin)
    mean_base = pi0 * base[0] + pi1 * base[1]
    c = core[0]
    for n, x in enumerate((density[...], margin, value[...], mean_base)):
        lo, hi = x[:HP], x[HP:]
        mine = jnp.where(c == 0, lo, hi)
        other = jnp.where(c == 0, hi, lo)
        for b in range(BPZ):
            keep[n, b] = mine[:, b * B : (b + 1) * B]
            send[n, b] = other[:, b * B : (b + 1) * B]


def k_pack(core, keep, recv, loc, pay):
    c = core[0]
    for n in range(4):
        for b in range(BPZ):
            k, r = keep[n, b], recv[n, b]
            loc[n, b] = jnp.where(c == 0, k, r)
            loc[n, BPZ + b] = jnp.where(c == 0, r, k)
    for b in range(ZB):
        hi, lo = split_parts(loc[1, b])
        dens = loc[0, b].astype(BF16)
        for z in range(pay.shape[0]):
            pay[z, 0, b] = dens
            pay[z, 1, b] = hi
            pay[z, 2, b] = lo


def arrivals(pay, acc, at, parts):
    for s in range(pay.shape[0]):
        put_sums(pay, s, at, [acc[s * ZB + b] for b in range(ZB)], parts)


def k1(core, own, oth, g, loc, t_own, t_oth, pi, pay, acc):
    for z in range(g.shape[0]):
        for b in range(ZB):
            m = g[z, 1, b].astype(F32) + g[z, 2, b].astype(F32)
            pi[0, z * ZB + b] = sigmoid(m)
            pi[1, z * ZB + b] = sigmoid(-m)
    forward(core[0], (own, oth), (t_own, t_oth), pi, lambda row: g[row // ZB, 0, row % ZB], acc)
    for b in range(ZB):
        put_all(pay, b, loc[2, b].astype(BF16))
    arrivals(pay, acc, ZB, PARTS[2])


def k2(core, own, oth, g, pi, t_own, t_oth, u1, pay, acc, rows):
    mass = jnp.zeros((HP, 1), F32)
    for b in range(ZB):
        u = get_sum(g, ZB, b, PARTS[2])
        u1[b] = u
        mass += jnp.sum(u, axis=1, keepdims=True)
        put_density(pay, 0, b, u, DENS[3])
    put_all(pay, DENS[3] * ZB, wide_parts(mass))
    acc[...] = jnp.zeros_like(acc)
    rows[...] = jnp.zeros_like(rows)

    def visit(a, row, r):
        acc[row] += pi[a, row] * r[:HP]
        rows[a, row] += r[HP:]

    backward(core[0], (own, oth), (t_own, t_oth), lambda col: g[col // ZB, col % ZB], visit, True)
    for z in range(pay.shape[0]):
        parts = [rows[a, z * ZB + b][0:1] for a in range(A) for b in range(ZB)]
        pay[z, DENS[3] * ZB + 1] = jnp.concatenate(parts, axis=0).astype(BF16)
        put_sums(pay, z, DENS[3] * ZB + 2, [acc[z * ZB + b] for b in range(ZB)], PARTS[3])


def k3(core, own, oth, g, pi, t_own, t_oth, lv, rsum, pay, acc):
    for b in range(ZB):
        lv[b] = discount * get_sum(g, DENS[3] * ZB + 2, b, PARTS[3])
    rsum[...] = jnp.sum(g[:, DENS[3] * ZB + 1].astype(F32), axis=0)
    put_all(pay, 0, wide_parts(narrow_parts(jnp.sum(g[:, DENS[3] * ZB].astype(F32), axis=0))))
    forward(core[0], (own, oth), (t_own, t_oth), pi, density_at(g, 0, DENS[3]), acc)
    arrivals(pay, acc, 1, PARTS[4])


def k4(n_states, g, loc, u1, rsum, u2, hs, pay):
    m1 = n_states / narrow_parts(jnp.sum(g[:, 0].astype(F32), axis=0))
    mass2 = jnp.zeros((HP, 1), F32)
    mass3 = jnp.zeros((HP, 1), F32)
    for b in range(ZB):
        u = get_sum(g, 1, b, PARTS[4]) * m1
        u2[b] = u
        hs[b : b + 1] = jnp.sum(u1[b] * m1, axis=0, keepdims=True)
        put_density(pay, 0, b, u, DENS[5])
        mass2 += jnp.sum(u, axis=1, keepdims=True)
        margin = loc[1, b]
        d = u.astype(BF16).astype(F32) if DENS[5] == 1 else u
        w0 = (sigmoid(margin) * d).astype(BF16).astype(F32)
        w1 = (sigmoid(-margin) * d).astype(BF16).astype(F32)
        per = w0 * rsum[b : b + 1] + w1 * rsum[ZB + b : ZB + b + 1]
        mass3 += jnp.sum(per, axis=1, keepdims=True)
    put_all(pay, DENS[5] * ZB, wide_parts(mass2))
    put_all(pay, DENS[5] * ZB + 1, wide_parts(mass3))


def k5(core, own, oth, g, pi, t_own, t_oth, pay, acc):
    for n in range(2):
        total = narrow_parts(jnp.sum(g[:, DENS[5] * ZB + n].astype(F32), axis=0))
        put_all(pay, n, wide_parts(total))
    forward(core[0], (own, oth), (t_own, t_oth), pi, density_at(g, 0, DENS[5]), acc)
    arrivals(pay, acc, 2, PARTS[6])


def k6(n_states, g, u2, hs1, d3, hs):
    m2 = n_states / narrow_parts(jnp.sum(g[:, 0].astype(F32), axis=0))
    m3 = n_states / narrow_parts(jnp.sum(g[:, 1].astype(F32), axis=0))
    for b in range(ZB):
        d = get_sum(g, 2, b, PARTS[6]) * m3
        d3[b] = d
        hs[b : b + 1] = hs1[b : b + 1]
        hs[ZB + b : ZB + b + 1] = jnp.sum(u2[b] * m2, axis=0, keepdims=True)
        hs[2 * ZB + b : 2 * ZB + b + 1] = jnp.sum(d, axis=0, keepdims=True)


def k7(hs, hs_oth, loc, lv, crowd, rew, pay):
    mean = (hs[...] + hs_oth[...]) * (1.0 / P_SIZE)
    crowding = jnp.log1p(mean)
    for n in range(3):
        for b in range(ZB):
            r = loc[3, b] - crowd[...] * crowding[n * ZB + b : n * ZB + b + 1]
            if n < 2:
                rew[n, b] = r
            else:
                put_all(pay, b, (r + lv[b]).astype(BF16))


def k8(core, own, oth, g, d3, pi, t_own, t_oth, pay, acc):
    acc[...] = jnp.zeros_like(acc)

    def visit(a, row, r):
        acc[row] += pi[a, row] * r

    backward(core[0], (own, oth), (t_own, t_oth), lambda col: g[col // ZB, col % ZB], visit)
    for b in range(ZB):
        put_density(pay, 0, b, d3[b], DENS[8])
    for z in range(pay.shape[0]):
        put_sums(pay, z, DENS[8] * ZB, [acc[z * ZB + b] for b in range(ZB)], PARTS[8])


def k9(core, own, oth, g, rew, pi, t_own, t_oth, pay, acc):
    for b in range(ZB):
        v = rew[1, b] + discount * get_sum(g, DENS[8] * ZB, b, PARTS[8])
        put_all(pay, b, v.astype(BF16))
    forward(core[0], (own, oth), (t_own, t_oth), pi, density_at(g, 0, DENS[8]), acc)
    arrivals(pay, acc, ZB, PARTS[9])


def k10(core, own, oth, g, pi, t_own, t_oth, u4, pay, acc):
    mass = jnp.zeros((HP, 1), F32)
    for b in range(ZB):
        u = get_sum(g, ZB, b, PARTS[9])
        u4[b] = u
        mass += jnp.sum(u, axis=1, keepdims=True)
    put_all(pay, 0, wide_parts(mass))
    acc[...] = jnp.zeros_like(acc)

    def visit(a, row, r):
        acc[row] += pi[a, row] * r

    backward(core[0], (own, oth), (t_own, t_oth), lambda col: g[col // ZB, col % ZB], visit)
    for z in range(pay.shape[0]):
        put_sums(pay, z, 1, [acc[z * ZB + b] for b in range(ZB)], PARTS[10])


def k11(g, rew, pay):
    for b in range(ZB):
        v = rew[0, b] + discount * get_sum(g, 1, b, PARTS[10])
        put_all(pay, b, v.astype(BF16))
    put_all(pay, ZB, wide_parts(narrow_parts(jnp.sum(g[:, 0].astype(F32), axis=0))))


def k12(n_states, core, own, oth, g, u4, t_own, t_oth, dkeep, dsend, pay, acc):
    c = core[0]
    m4 = n_states / narrow_parts(jnp.sum(g[:, ZB].astype(F32), axis=0))
    for b in range(BPZ):
        x, y = u4[b] * m4, u4[BPZ + b] * m4
        dkeep[b] = jnp.where(c == 0, x, y)
        dsend[b] = jnp.where(c == 0, y, x)
    acc[...] = jnp.zeros_like(acc)

    def visit(a, row, r):
        acc[a, row] += r

    backward(c, (own, oth), (t_own, t_oth), lambda col: g[col // ZB, col % ZB], visit)
    for z in range(pay.shape[0]):
        put_sums(pay, z, 0, [acc[a, z * ZB + b] for a in range(A) for b in range(ZB)], PARTS[12])


def k13(core, g, keep, send):
    c = core[0]
    for a in range(A):
        for b in range(BPZ):
            x = get_sum(g, 0, a * ZB + b, PARTS[12])
            y = get_sum(g, 0, a * ZB + BPZ + b, PARTS[12])
            keep[a, b] = jnp.where(c == 0, x, y)
            send[a, b] = jnp.where(c == 0, y, x)


def k14(core, keep, recv, dkeep, drecv, density, logits, base, crowd, new_logits, value, final):
    c = core[0]
    mean = jnp.sum(density[...], axis=0, keepdims=True) * (1.0 / P_SIZE)
    bite = crowd[...] * jnp.log1p(mean)
    margin = logits[0] - logits[1]
    pis = (sigmoid(margin), sigmoid(-margin))

    def whole(k, r):
        first = jnp.concatenate([k[b] for b in range(BPZ)], axis=1)
        second = jnp.concatenate([r[b] for b in range(BPZ)], axis=1)
        lo = jnp.where(c == 0, first, second)
        hi = jnp.where(c == 0, second, first)
        return jnp.concatenate([lo, hi], axis=0)

    total = jnp.zeros_like(margin)
    for a in range(A):
        av = base[a] - bite + discount * whole(keep[a], recv[a])
        new_logits[a] = logits[a] + step_size * av
        total += pis[a] * av
    value[...] = total
    final[...] = whole(dkeep, drecv)


def body(density0, logits, value_final, base_reward, crowd, tiles, tile_src, tile_dst, tile_count):
    ns = lax.axis_size("src")
    nd = lax.axis_size("dst")
    nz = nd // 2
    n_states = float(density0.shape[1] * ns * nd)
    swap = [(i, i ^ 1) for i in range(nd)]
    groups = [[2 * z + c for z in range(nz)] for c in range(2)]
    core = (lax.axis_index("dst") % 2).astype(jnp.int32)
    core1 = core[None]
    my_crowd = jnp.broadcast_to(lax.dynamic_slice(crowd, (core * HP,), (HP,))[:, None], (HP, B))
    all_crowd = jnp.broadcast_to(crowd[:, None], (P_SIZE, BPZ * B))

    def other(x):
        return lax.ppermute(x, "dst", swap)

    def over_z(x):
        return lax.all_to_all(x, "dst", 0, 0, tiled=True, axis_index_groups=groups)

    def over_src(x):
        return lax.all_to_all(x, "src", 0, 0, tiled=True)

    t_own = tiles.reshape(A * TCAP, B, B)
    own = jnp.concatenate([tile_src.reshape(-1), tile_dst.reshape(-1), tile_count.reshape(-1)])
    send, keep = call(
        lambda core, density, logits, base, value, send, keep: k_start(density, logits, base, value, core, send, keep),
        [((4, BPZ, HP, B), F32)] * 2,
        1,
    )(core1, density0, logits, base_reward, value_final)
    recv = other(send)
    oth = other(own)
    t_oth = other(t_own)
    loc, pay1 = call(k_pack, [((4, ZB, HP, B), F32), ((nz, 3, ZB, HP, B), BF16)], 1)(core1, keep, recv)
    ix = (core1, own, oth)
    tt = (t_own, t_oth)
    fwd = [pltpu.VMEM((ns * ZB, HP, B), F32)]
    bwd = [pltpu.VMEM((nz * ZB, HP, B), F32)]
    g1 = over_z(pay1)
    pi, pay2 = call(k1, [((A, nz * ZB, HP, B), F32), ((ns, ZB + PARTS[2] * ZB, HP, B), BF16)], 3, fwd)(*ix, g1, loc, *tt)
    g2 = over_src(pay2)
    rows = [pltpu.VMEM((A, nz * ZB, HP, B), F32)]
    u1, pay3 = call(k2, [((ZB, HP, B), F32), ((nz, DENS[3] * ZB + 2 + PARTS[3] * ZB, HP, B), BF16)], 3, bwd + rows)(*ix, g2, pi, *tt)
    g3 = over_z(pay3)
    lv, rsum, pay4 = call(k3, [((ZB, HP, B), F32), ((HP, B), F32), ((ns, 1 + PARTS[4] * ZB, HP, B), BF16)], 3, fwd)(
        *ix, g3, pi, *tt
    )
    g4 = over_src(pay4)
    u2, hs1, pay5 = call(
        lambda *r: k4(n_states, *r), [((ZB, HP, B), F32), ((ZB, B), F32), ((nz, DENS[5] * ZB + 2, HP, B), BF16)], 0
    )(g4, loc, u1, rsum)
    g5 = over_z(pay5)
    (pay6,) = call(k5, [((ns, 2 + PARTS[6] * ZB, HP, B), BF16)], 3, fwd)(*ix, g5, pi, *tt)
    g6 = over_src(pay6)
    d3, hs = call(lambda *r: k6(n_states, *r), [((ZB, HP, B), F32), ((3 * ZB, B), F32)], 0)(g6, u2, hs1)
    hs_oth = other(hs)
    rew, pay7 = call(k7, [((2, ZB, HP, B), F32), ((ns, ZB, HP, B), BF16)], 0)(hs, hs_oth, loc, lv, my_crowd)
    g7 = over_src(pay7)
    (pay8,) = call(k8, [((nz, DENS[8] * ZB + PARTS[8] * ZB, HP, B), BF16)], 3, bwd)(*ix, g7, d3, pi, *tt)
    g8 = over_z(pay8)
    (pay9,) = call(k9, [((ns, ZB + PARTS[9] * ZB, HP, B), BF16)], 3, fwd)(*ix, g8, rew, pi, *tt)
    g9 = over_src(pay9)
    u4, pay10 = call(k10, [((ZB, HP, B), F32), ((nz, 1 + PARTS[10] * ZB, HP, B), BF16)], 3, bwd)(*ix, g9, pi, *tt)
    g10 = over_z(pay10)
    (pay11,) = call(k11, [((ns, ZB + 1, HP, B), BF16)], 0)(g10, rew)
    g11 = over_src(pay11)
    dkeep, dsend, pay12 = call(
        lambda *r: k12(n_states, *r),
        [((BPZ, HP, B), F32), ((BPZ, HP, B), F32), ((nz, PARTS[12] * A * ZB, HP, B), BF16)],
        3,
        [pltpu.VMEM((A, nz * ZB, HP, B), F32)],
    )(*ix, g11, u4, *tt)
    drecv = other(dsend)
    g12 = over_z(pay12)
    rkeep, rsend = call(k13, [((A, BPZ, HP, B), F32)] * 2, 1)(core1, g12)
    rrecv = other(rsend)
    new_logits, value, final = call(
        k14,
        [(logits.shape, F32), (density0.shape, F32), (density0.shape, F32)],
        1,
    )(core1, rkeep, rrecv, dkeep, drecv, density0, logits, base_reward, all_crowd)
    return (new_logits, value, final)


def solution(mesh):
    in_specs = (
        P(None, ("src", "dst")),
        P(None, None, ("src", "dst")),
        P(None, ("src", "dst")),
        P(None, None, ("src", "dst")),
        P(),
        P("src", "dst", None, None, None, None),
        P("src", "dst", None, None),
        P("src", "dst", None, None),
        P("src", "dst", None),
    )
    out_specs = (P(None, None, ("src", "dst")), P(None, ("src", "dst")), P(None, ("src", "dst")))
    return jax.shard_map(body, mesh=mesh, in_specs=in_specs, out_specs=out_specs, check_vma=False)
```

```python
import jax
import jax.numpy as jnp
from jax import lax
from jax.experimental import pallas as pl
from jax.experimental.pallas import tpu as pltpu
from jax.sharding import PartitionSpec as P


P_SIZE = 16
A = 2
B = 256
BPZ = 2
TCAP = 8
H = 4

HP = P_SIZE // 2
ZB = 2 * BPZ

discount = 0.9
step_size = 1.0

F32 = jnp.float32
BF16 = jnp.bfloat16


def sigmoid(v):
    return 1.0 / (1.0 + jnp.exp(-v))


def split_parts(x):
    hi = x.astype(BF16)
    lo = (x - hi.astype(F32)).astype(BF16)
    return hi, lo


def wide_parts(col):
    hi, lo = split_parts(jnp.broadcast_to(col, (HP, B // 2)))
    return jnp.concatenate([hi, lo], axis=1)


def narrow_parts(block):
    return block[:, 0:1] + block[:, B // 2 : B // 2 + 1]


I16 = jnp.int16
TOP = 32766.0
LOG = 0.6931471805599453 / 128.0
DENSITY_UNIT = 5.0 / TOP
MARGIN_UNIT = 12.0 / TOP


def coded(x):
    return jnp.floor(x + 0.5).astype(jnp.int32).astype(I16)


def unit_of(k):
    return jnp.exp(k * LOG) * (1.0 / TOP)


def row_code(x):
    top = jnp.max(jnp.abs(x), axis=1, keepdims=True)
    k = jnp.ceil(jnp.log(jnp.maximum(top, 1e-37)) * (1.0 / LOG)) + 1.0
    return x * (1.0 / unit_of(k)), k


def pack_cols(cols):
    lane = lax.broadcasted_iota(jnp.int32, (HP, B), 1) // 16
    block = jnp.zeros((HP, B), F32)
    for n, col in enumerate(cols):
        block = jnp.where(lane == n, col, block)
    return coded(block)


def col_of(block, n):
    return block[:, 16 * n : 16 * n + 1]


def mass_cols(mass):
    y, k = row_code(mass)
    whole = jnp.floor(y)
    return [k, whole, (y - whole) * TOP]


def mass_of(block, n):
    y = col_of(block, n + 1) + col_of(block, n + 2) * (1.0 / TOP)
    return y * unit_of(col_of(block, n))


def put_coded(ref, peer, blocks, more=()):
    cols = []
    for b, x in enumerate(blocks):
        y, k = row_code(x)
        ref[peer, 1 + b] = coded(y)
        cols.append(k)
    ref[peer, 0] = pack_cols(cols + list(more))


def get_coded(ref, blocks):
    totals = [jnp.zeros((HP, B), F32) for _ in range(blocks)]
    for peer in range(ref.shape[0]):
        unit = unit_of(ref[peer, 0].astype(F32))
        for b in range(blocks):
            totals[b] += ref[peer, 1 + b].astype(F32) * col_of(unit, b)
    return totals


def call(kernel, outs, n_smem, scratch=(), n_any=0, limit=12 << 20):
    def run(*args):
        specs = [pl.BlockSpec(memory_space=pltpu.SMEM)] * n_smem
        specs += [pl.BlockSpec(memory_space=pltpu.VMEM)] * (len(args) - n_smem - n_any)
        specs += [pl.BlockSpec(memory_space=pl.ANY)] * n_any
        return pl.pallas_call(
            kernel,
            out_shape=[jax.ShapeDtypeStruct(s, d) for s, d in outs],
            in_specs=specs,
            out_specs=[pl.BlockSpec(memory_space=pltpu.VMEM)] * len(outs),
            scratch_shapes=list(scratch),
            compiler_params=pltpu.CompilerParams(vmem_limit_bytes=limit),
        )(*args)

    return run


def slots(core, idx_refs, tile_refs):
    for which in range(2):
        origin = core if which == 0 else 1 - core
        idx = idx_refs[which]
        for a in range(A):
            count = idx[0, 0, a, 2 * TCAP]
            for k in range(TCAP):
                row = idx[0, 0, a, k]
                dst = idx[0, 0, a, TCAP + k]
                col = (dst // BPZ) * ZB + origin * BPZ + dst % BPZ
                live = (k < count).astype(F32)
                yield a, row, col, live, tile_refs[which], a * TCAP + k


def forward(core, idx_refs, tile_refs, pi_ref, dens_of, acc, ready=None):
    acc[...] = jnp.zeros_like(acc)
    for n, (a, row, col, live, tiles, k) in enumerate(slots(core, idx_refs, tile_refs)):
        if ready is not None:
            ready(n)
        w = (pi_ref[a, row] * (dens_of(row) * live)).astype(BF16)
        acc[col] += jnp.dot(w, tiles[k], preferred_element_type=F32)


def backward(core, idx_refs, tile_refs, v_of, visit, ones=False):
    for a, row, col, live, tiles, k in slots(core, idx_refs, tile_refs):
        v = v_of(col)
        if ones:
            v = jnp.concatenate([v, jnp.ones((HP, B), BF16)], axis=0)
        r = lax.dot_general(v, tiles[k], (((1,), (1,)), ((), ())), preferred_element_type=F32)
        visit(a, row, r * live)


PARTS = {2: 1, 3: 1, 4: 1, 10: 1}

DENS = {3: 1}


def put_density(ref, at, b, x, parts):
    if parts == 1:
        put_all(ref, at + b, x.astype(BF16))
    else:
        hi, lo = split_parts(x)
        put_all(ref, at + 2 * b, hi)
        put_all(ref, at + 2 * b + 1, lo)


def density_at(ref, at, parts):
    def get(row):
        z, b = row // ZB, at + parts * (row % ZB)
        if parts == 1:
            return ref[z, b].astype(F32)
        return ref[z, b].astype(F32) + ref[z, b + 1].astype(F32)

    return get


def put_sums(ref, peer, at, blocks, parts):
    for b, x in enumerate(blocks):
        if parts == 1:
            ref[peer, at + b] = x.astype(BF16)
        else:
            hi, lo = split_parts(x)
            ref[peer, at + 2 * b] = hi
            ref[peer, at + 2 * b + 1] = lo


def get_sum(ref, at, b, parts):
    total = jnp.sum(ref[:, at + parts * b].astype(F32), axis=0)
    if parts == 2:
        total += jnp.sum(ref[:, at + 2 * b + 1].astype(F32), axis=0)
    return total


def put_all(ref, at, block):
    for peer in range(ref.shape[0]):
        ref[peer, at] = block


def k_start(density, logits, pay):
    margin = logits[0] - logits[1]
    for n, x in enumerate((coded(density[...] * (1.0 / DENSITY_UNIT)), coded(margin * (1.0 / MARGIN_UNIT)))):
        for b in range(BPZ):
            for c in range(2):
                block = x[c * HP : (c + 1) * HP, b * B : (b + 1) * B]
                for d in range(c, pay.shape[0], 2):
                    pay[d, n, b] = block


def rows_of(scalars):
    return jnp.concatenate([jnp.full((1, B), x, F32) for x in scalars], axis=0)


def arrivals(pay, acc, at, parts):
    for s in range(pay.shape[0]):
        put_sums(pay, s, at, [acc[s * ZB + b] for b in range(ZB)], parts)


def k1(at, own, oth, g, keep, recv, t_own, t_oth, pi, loc, pay, acc):
    c = at[0]
    for d in range(g.shape[0]):
        for b in range(BPZ):
            m = g[d, 1, b].astype(F32) * MARGIN_UNIT
            pi[0, d * BPZ + b] = sigmoid(m)
            pi[1, d * BPZ + b] = sigmoid(-m)
    for n in range(2):
        for b in range(BPZ):
            k, r = keep[n, :, b * B : (b + 1) * B], recv[n, :, b * B : (b + 1) * B]
            loc[n, b] = jnp.where(c == 0, k, r)
            loc[n, BPZ + b] = jnp.where(c == 0, r, k)
    for b in range(ZB):
        put_all(pay, b, loc[0, b].astype(BF16))

    def dens_of(row):
        return g[row // BPZ, 0, row % BPZ].astype(F32) * DENSITY_UNIT

    forward(c, (own, oth), (t_own, t_oth), pi, dens_of, acc)
    arrivals(pay, acc, ZB, PARTS[2])


def k2(core, own, oth, g, pi, t_own, t_oth, u1, pay, acc, rows):
    mass = jnp.zeros((HP, 1), F32)
    for b in range(ZB):
        u = get_sum(g, ZB, b, PARTS[2])
        u1[b] = u
        mass += jnp.sum(u, axis=1, keepdims=True)
        put_density(pay, 0, b, u, DENS[3])
    put_all(pay, DENS[3] * ZB, wide_parts(mass))
    acc[...] = jnp.zeros_like(acc)
    rows[...] = jnp.zeros_like(rows)

    def visit(a, row, r):
        acc[row] += pi[a, row] * r[:HP]
        rows[a, row] += r[HP:]

    backward(core[0], (own, oth), (t_own, t_oth), lambda col: g[col // ZB, col % ZB], visit, True)
    for z in range(pay.shape[0]):
        parts = [rows[a, z * ZB + b][0:1] for a in range(A) for b in range(ZB)]
        pay[z, DENS[3] * ZB + 1] = jnp.concatenate(parts, axis=0).astype(BF16)
        put_sums(pay, z, DENS[3] * ZB + 2, [acc[z * ZB + b] for b in range(ZB)], PARTS[3])


def k3(core, own, oth, g, pi, t_own, t_oth, lv, rsum, pay, acc):
    for b in range(ZB):
        lv[b] = discount * get_sum(g, DENS[3] * ZB + 2, b, PARTS[3])
    rsum[...] = jnp.sum(g[:, DENS[3] * ZB + 1].astype(F32), axis=0)
    put_all(pay, 0, wide_parts(narrow_parts(jnp.sum(g[:, DENS[3] * ZB].astype(F32), axis=0))))
    forward(core[0], (own, oth), (t_own, t_oth), pi, density_at(g, 0, DENS[3]), acc)
    arrivals(pay, acc, 1, PARTS[4])


def k4(n_states, at, g, pi, u1, rsum, u2, hs, pay):
    m1 = n_states / narrow_parts(jnp.sum(g[:, 0].astype(F32), axis=0))
    mass2 = jnp.zeros((HP, 1), F32)
    mass3 = jnp.zeros((HP, 1), F32)
    cols = []
    for b in range(ZB):
        u = get_sum(g, 1, b, PARTS[4]) * m1
        u2[b] = u
        hs[b : b + 1] = jnp.sum(u1[b] * m1, axis=0, keepdims=True)
        y, k = row_code(u)
        put_all(pay, 1 + b, coded(y))
        cols.append(k)
        mass2 += jnp.sum(u, axis=1, keepdims=True)
        row = at[1] * ZB + b
        w0 = (pi[0, row] * u).astype(BF16).astype(F32)
        w1 = (pi[1, row] * u).astype(BF16).astype(F32)
        per = w0 * rsum[b : b + 1] + w1 * rsum[ZB + b : ZB + b + 1]
        mass3 += jnp.sum(per, axis=1, keepdims=True)
    put_all(pay, 0, pack_cols(cols + mass_cols(mass2) + mass_cols(mass3)))


def k5(core, own, oth, g, pi, t_own, t_oth, pay, acc, dens):
    masses = [jnp.zeros((HP, 1), F32), jnp.zeros((HP, 1), F32)]
    for z in range(g.shape[0]):
        block = g[z, 0].astype(F32)
        for n in range(2):
            masses[n] += mass_of(block, ZB + 3 * n)
        unit = unit_of(block)
        for b in range(ZB):
            dens[z * ZB + b] = g[z, 1 + b].astype(F32) * col_of(unit, b)
    more = mass_cols(masses[0]) + mass_cols(masses[1])
    forward(core[0], (own, oth), (t_own, t_oth), pi, lambda row: dens[row], acc)
    for s in range(pay.shape[0]):
        put_coded(pay, s, [acc[s * ZB + b] for b in range(ZB)], more)


def k6(n_states, g, u2, hs1, d3, hs):
    mass2 = jnp.zeros((HP, 1), F32)
    mass3 = jnp.zeros((HP, 1), F32)
    for peer in range(g.shape[0]):
        block = g[peer, 0].astype(F32)
        mass2 += mass_of(block, ZB)
        mass3 += mass_of(block, ZB + 3)
    m2, m3 = n_states / mass2, n_states / mass3
    totals = get_coded(g, ZB)
    for b in range(ZB):
        d = totals[b] * m3
        d3[b] = d
        hs[b : b + 1] = hs1[b : b + 1]
        hs[ZB + b : ZB + b + 1] = jnp.sum(u2[b] * m2, axis=0, keepdims=True)
        hs[2 * ZB + b : 2 * ZB + b + 1] = jnp.sum(d, axis=0, keepdims=True)


def k7(at, crowd, hs, hs_oth, loc, lv, rew, pay):
    crowd_rows = rows_of([crowd[at[0] * HP + p] for p in range(HP)])
    mean = (hs[...] + hs_oth[...]) * (1.0 / P_SIZE)
    crowding = jnp.log1p(mean)
    for n in range(3):
        for b in range(ZB):
            r = loc[1, b] - crowd_rows * crowding[n * ZB + b : n * ZB + b + 1]
            if n < 2:
                rew[n, b] = r
            else:
                put_all(pay, b, (r + lv[b]).astype(BF16))


def k8(core, own, oth, g, d3, pi, t_own, t_oth, pay, acc):
    acc[...] = jnp.zeros_like(acc)

    def visit(a, row, r):
        acc[row] += pi[a, row] * r

    backward(core[0], (own, oth), (t_own, t_oth), lambda col: g[col // ZB, col % ZB], visit)
    cols = []
    for b in range(ZB):
        y, k = row_code(d3[b])
        put_all(pay, 1 + ZB + b, coded(y))
        cols.append(k)
    for z in range(pay.shape[0]):
        put_coded(pay, z, [acc[z * ZB + b] for b in range(ZB)], cols)


def k9(core, own, oth, g, rew, pi, t_own, t_oth, pay, acc, dens):
    totals = get_coded(g, ZB)
    cols = []
    for b in range(ZB):
        v = rew[1, b] + discount * totals[b]
        y, k = row_code(v)
        put_all(pay, 1 + ZB + b, coded(y))
        cols.append(k)
    for z in range(g.shape[0]):
        unit = unit_of(g[z, 0].astype(F32))
        for b in range(ZB):
            dens[z * ZB + b] = g[z, 1 + ZB + b].astype(F32) * col_of(unit, ZB + b)
    forward(core[0], (own, oth), (t_own, t_oth), pi, lambda row: dens[row], acc)
    for s in range(pay.shape[0]):
        put_coded(pay, s, [acc[s * ZB + b] for b in range(ZB)], cols)


def k10(core, own, oth, g, pi, t_own, t_oth, u4, pay, acc, vals):
    mass = jnp.zeros((HP, 1), F32)
    totals = get_coded(g, ZB)
    for b in range(ZB):
        u4[b] = totals[b]
        mass += jnp.sum(totals[b], axis=1, keepdims=True)
    for s in range(g.shape[0]):
        unit = unit_of(g[s, 0].astype(F32))
        for b in range(ZB):
            vals[s * ZB + b] = (g[s, 1 + ZB + b].astype(F32) * col_of(unit, ZB + b)).astype(BF16)
    put_all(pay, 0, wide_parts(mass))
    acc[...] = jnp.zeros_like(acc)

    def visit(a, row, r):
        acc[row] += pi[a, row] * r

    backward(core[0], (own, oth), (t_own, t_oth), lambda col: vals[col], visit)
    for z in range(pay.shape[0]):
        put_sums(pay, z, 1, [acc[z * ZB + b] for b in range(ZB)], PARTS[10])


def k11(g, rew, pay):
    for b in range(ZB):
        v = rew[0, b] + discount * get_sum(g, 1, b, PARTS[10])
        put_all(pay, b, v.astype(BF16))
    put_all(pay, ZB, wide_parts(narrow_parts(jnp.sum(g[:, 0].astype(F32), axis=0))))


def k12(n_states, core, own, oth, g, u4, t_own, t_oth, dkeep, dsend, pay, acc):
    c = core[0]
    m4 = n_states / narrow_parts(jnp.sum(g[:, ZB].astype(F32), axis=0))
    for b in range(BPZ):
        x, y = u4[b] * m4, u4[BPZ + b] * m4
        dkeep[b] = jnp.where(c == 0, x, y)
        dsend[b] = jnp.where(c == 0, y, x)
    acc[...] = jnp.zeros_like(acc)

    def visit(a, row, r):
        acc[a, row] += r

    backward(c, (own, oth), (t_own, t_oth), lambda col: g[col // ZB, col % ZB], visit)
    for z in range(pay.shape[0]):
        put_coded(pay, z, [acc[a, z * ZB + b] for a in range(A) for b in range(ZB)])


def k13(at, g, keep, send):
    c = at[0]
    totals = get_coded(g, A * ZB)
    for a in range(A):
        for b in range(BPZ):
            x, y = totals[a * ZB + b], totals[a * ZB + BPZ + b]
            keep[a, b] = jnp.where(c == 0, x, y)
            send[a, b] = jnp.where(c == 0, y, x)


def k14(at, crowd, keep, recv, dkeep, drecv, density, logits, base, new_logits, value, final):
    c = at[0]
    mean = jnp.sum(density[...], axis=0, keepdims=True) * (1.0 / P_SIZE)
    crowd_rows = rows_of([crowd[p] for p in range(P_SIZE)])
    bite = jnp.concatenate([crowd_rows] * BPZ, axis=1) * jnp.log1p(mean)
    margin = logits[0] - logits[1]
    pis = (sigmoid(margin), sigmoid(-margin))

    def whole(k, r):
        first = jnp.concatenate([k[b] for b in range(BPZ)], axis=1)
        second = jnp.concatenate([r[b] for b in range(BPZ)], axis=1)
        lo = jnp.where(c == 0, first, second)
        hi = jnp.where(c == 0, second, first)
        return jnp.concatenate([lo, hi], axis=0)

    total = jnp.zeros_like(margin)
    for a in range(A):
        av = base[a] - bite + discount * whole(keep[a], recv[a])
        new_logits[a] = logits[a] + step_size * av
        total += pis[a] * av
    value[...] = total
    final[...] = whole(dkeep, drecv)


def body(density0, logits, value_final, base_reward, crowd, tiles, tile_src, tile_dst, tile_count):
    ns = lax.axis_size("src")
    nd = lax.axis_size("dst")
    nz = nd // 2
    n_states = float(density0.shape[1] * ns * nd)
    swap = [(i, i ^ 1) for i in range(nd)]
    groups = [[2 * z + c for z in range(nz)] for c in range(2)]
    me = lax.axis_index("dst").astype(jnp.int32)
    core1 = jnp.stack([me % 2, me // 2])

    def other(x):
        return lax.ppermute(x, "dst", swap)

    def over_z(x):
        return lax.all_to_all(x, "dst", 0, 0, tiled=True, axis_index_groups=groups)

    def over_src(x):
        return lax.all_to_all(x, "src", 0, 0, tiled=True)

    t_own = tiles.reshape(A * TCAP, B, B)
    (pay1,) = call(k_start, [((nd, 2, BPZ, HP, B), I16)], 0)(density0, logits)
    own = jnp.concatenate([tile_src, tile_dst, tile_count[..., None]], axis=3)
    margin = logits[0] - logits[1]
    mean_base = sigmoid(margin) * base_reward[0] + sigmoid(-margin) * base_reward[1]
    both = jnp.stack([value_final, mean_base])
    send = lax.dynamic_slice(both, (0, (1 - core1[0]) * HP, 0), (2, HP, BPZ * B))
    keep = lax.dynamic_slice(both, (0, core1[0] * HP, 0), (2, HP, BPZ * B))
    oth = other(own)
    recv = other(send)
    t_oth = other(t_own)
    ix = (core1, own, oth)
    tt = (t_own, t_oth)
    fwd = [pltpu.VMEM((ns * ZB, HP, B), F32)]
    bwd = [pltpu.VMEM((nz * ZB, HP, B), F32)]
    dens = [pltpu.VMEM((nz * ZB, HP, B), F32)]
    vals = [pltpu.VMEM((ns * ZB, HP, B), BF16)]
    g1 = lax.all_to_all(pay1, "dst", 0, 0, tiled=True)
    pi, loc, pay2 = call(
        k1,
        [((A, nz * ZB, HP, B), F32), ((2, ZB, HP, B), F32), ((ns, ZB + PARTS[2] * ZB, HP, B), BF16)],
        3,
        fwd,
    )(*ix, g1, keep, recv, *tt)
    g2 = over_src(pay2)
    rows = [pltpu.VMEM((A, nz * ZB, HP, B), F32)]
    u1, pay3 = call(k2, [((ZB, HP, B), F32), ((nz, DENS[3] * ZB + 2 + PARTS[3] * ZB, HP, B), BF16)], 3, bwd + rows)(*ix, g2, pi, *tt)
    g3 = over_z(pay3)
    lv, rsum, pay4 = call(k3, [((ZB, HP, B), F32), ((HP, B), F32), ((ns, 1 + PARTS[4] * ZB, HP, B), BF16)], 3, fwd)(
        *ix, g3, pi, *tt
    )
    g4 = over_src(pay4)
    u2, hs1, pay5 = call(
        lambda *r: k4(n_states, *r), [((ZB, HP, B), F32), ((ZB, B), F32), ((nz, 1 + ZB, HP, B), I16)], 1
    )(core1, g4, pi, u1, rsum)
    g5 = over_z(pay5)
    (pay6,) = call(k5, [((ns, 1 + ZB, HP, B), I16)], 3, fwd + dens)(*ix, g5, pi, *tt)
    g6 = over_src(pay6)
    d3, hs = call(lambda *r: k6(n_states, *r), [((ZB, HP, B), F32), ((3 * ZB, B), F32)], 0)(g6, u2, hs1)
    hs_oth = other(hs)
    rew, pay7 = call(k7, [((2, ZB, HP, B), F32), ((ns, ZB, HP, B), BF16)], 2)(core1, crowd, hs, hs_oth, loc, lv)
    g7 = over_src(pay7)
    (pay8,) = call(k8, [((nz, 1 + 2 * ZB, HP, B), I16)], 3, bwd)(*ix, g7, d3, pi, *tt)
    g8 = over_z(pay8)
    (pay9,) = call(k9, [((ns, 1 + 2 * ZB, HP, B), I16)], 3, fwd + dens)(*ix, g8, rew, pi, *tt)
    g9 = over_src(pay9)
    u4, pay10 = call(k10, [((ZB, HP, B), F32), ((nz, 1 + PARTS[10] * ZB, HP, B), BF16)], 3, bwd + vals)(*ix, g9, pi, *tt)
    g10 = over_z(pay10)
    (pay11,) = call(k11, [((ns, ZB + 1, HP, B), BF16)], 0)(g10, rew)
    g11 = over_src(pay11)
    dkeep, dsend, pay12 = call(
        lambda *r: k12(n_states, *r),
        [((BPZ, HP, B), F32), ((BPZ, HP, B), F32), ((nz, 1 + A * ZB, HP, B), I16)],
        3,
        [pltpu.VMEM((A, nz * ZB, HP, B), F32)],
    )(*ix, g11, u4, *tt)
    drecv = other(dsend)
    g12 = over_z(pay12)
    rkeep, rsend = call(k13, [((A, BPZ, HP, B), F32)] * 2, 1)(core1, g12)
    rrecv = other(rsend)
    new_logits, value, final = call(
        k14,
        [(logits.shape, F32), (density0.shape, F32), (density0.shape, F32)],
        2,
    )(core1, crowd, rkeep, rrecv, dkeep, drecv, density0, logits, base_reward)
    return (new_logits, value, final)


def solution(mesh):
    in_specs = (
        P(None, ("src", "dst")),
        P(None, None, ("src", "dst")),
        P(None, ("src", "dst")),
        P(None, None, ("src", "dst")),
        P(),
        P("src", "dst", None, None, None, None),
        P("src", "dst", None, None),
        P("src", "dst", None, None),
        P("src", "dst", None),
    )
    out_specs = (P(None, None, ("src", "dst")), P(None, ("src", "dst")), P(None, ("src", "dst")))
    return jax.shard_map(body, mesh=mesh, in_specs=in_specs, out_specs=out_specs, check_vma=False)
```

```python
import jax
import jax.numpy as jnp
from jax import lax
from jax.experimental import pallas as pl
from jax.experimental.pallas import tpu as pltpu
from jax.sharding import PartitionSpec as P


P_SIZE = 16
A = 2
B = 256
BPZ = 2
TCAP = 8
H = 4

HP = P_SIZE // 2
ZB = 2 * BPZ

discount = 0.9
step_size = 1.0

F32 = jnp.float32
BF16 = jnp.bfloat16


def sigmoid(v):
    return 1.0 / (1.0 + jnp.exp(-v))


HW = B // 2


def split_parts(x):
    hi = x.astype(BF16)
    lo = (x - hi.astype(F32)).astype(BF16)
    return hi, lo


def wide_parts(col):
    hi, lo = split_parts(jnp.broadcast_to(col, (HP, HW // 2)))
    return jnp.concatenate([hi, lo], axis=1)


def mass_total(ref):
    block = jnp.sum(ref[:, 0].astype(F32), axis=0)
    return block[:, 0:1] + block[:, HW // 2 : HW // 2 + 1]


I16 = jnp.int16
TOP = 32766.0
LOG = 0.6931471805599453 / 128.0
DENSITY_UNIT = 5.0 / TOP
MARGIN_UNIT = 12.0 / TOP


def coded(x):
    return jnp.floor(x + 0.5).astype(jnp.int32).astype(I16)


def unit_of(k):
    return jnp.exp(k * LOG) * (1.0 / TOP)


def row_code(x):
    top = jnp.max(jnp.abs(x), axis=1, keepdims=True)
    k = jnp.ceil(jnp.log(jnp.maximum(top, 1e-37)) * (1.0 / LOG)) + 1.0
    return x * (1.0 / unit_of(k)), k


def pack_cols(cols):
    lane = lax.broadcasted_iota(jnp.int32, (HP, HW), 1) // 8
    block = jnp.zeros((HP, HW), F32)
    for n, col in enumerate(cols):
        block = jnp.where(lane == n, col, block)
    return coded(block)


def col_of(block, n):
    return block[:, 8 * n : 8 * n + 1]


def mass_cols(mass):
    y, k = row_code(mass)
    whole = jnp.floor(y)
    return [k, whole, (y - whole) * TOP]


def mass_of(block, n):
    y = col_of(block, n + 1) + col_of(block, n + 2) * (1.0 / TOP)
    return y * unit_of(col_of(block, n))


def put(ref, peer, b, block):
    if ref.shape[-1] == B:
        ref[peer, b] = block
    else:
        ref[peer, 1 + 2 * b] = block[:, :HW]
        ref[peer, 2 + 2 * b] = block[:, HW:]


def load(ref, peer, b):
    if ref.shape[-1] == B:
        return ref[peer, b]
    return jnp.concatenate([ref[peer, 1 + 2 * b], ref[peer, 2 + 2 * b]], axis=1)


def put_all(ref, b, block):
    for peer in range(ref.shape[0]):
        put(ref, peer, b, block)


def put_heads(ref, block):
    for peer in range(ref.shape[0]):
        ref[peer, 0] = block


def get_sum(ref, b):
    if ref.shape[-1] == B:
        return jnp.sum(ref[:, b].astype(F32), axis=0)
    halves = [jnp.sum(ref[:, 1 + 2 * b + n].astype(F32), axis=0) for n in range(2)]
    return jnp.concatenate(halves, axis=1)


def put_coded(ref, peer, blocks, more=()):
    cols = []
    for b, x in enumerate(blocks):
        y, k = row_code(x)
        put(ref, peer, b, coded(y))
        cols.append(k)
    ref[peer, 0] = pack_cols(cols + list(more))


def get_coded(ref, blocks):
    totals = [jnp.zeros((HP, B), F32) for _ in range(blocks)]
    for peer in range(ref.shape[0]):
        unit = unit_of(ref[peer, 0].astype(F32))
        for b in range(blocks):
            totals[b] += load(ref, peer, b).astype(F32) * col_of(unit, b)
    return totals


def call(kernel, outs, n_smem, scratch=(), n_any=0, limit=12 << 20):
    def run(*args):
        specs = [pl.BlockSpec(memory_space=pltpu.SMEM)] * n_smem
        specs += [pl.BlockSpec(memory_space=pltpu.VMEM)] * (len(args) - n_smem - n_any)
        specs += [pl.BlockSpec(memory_space=pl.ANY)] * n_any
        return pl.pallas_call(
            kernel,
            out_shape=[jax.ShapeDtypeStruct(s, d) for s, d in outs],
            in_specs=specs,
            out_specs=[pl.BlockSpec(memory_space=pltpu.VMEM)] * len(outs),
            scratch_shapes=list(scratch),
            compiler_params=pltpu.CompilerParams(vmem_limit_bytes=limit),
        )(*args)

    return run


def slots(core, idx_refs, tile_refs):
    for which in range(2):
        origin = core if which == 0 else 1 - core
        idx = idx_refs[which]
        for a in range(A):
            count = idx[0, 0, a, 2 * TCAP]
            for k in range(TCAP):
                row = idx[0, 0, a, k]
                dst = idx[0, 0, a, TCAP + k]
                col = (dst // BPZ) * ZB + origin * BPZ + dst % BPZ
                live = (k < count).astype(F32)
                yield a, row, col, live, tile_refs[which], a * TCAP + k


def forward(core, idx_refs, tile_refs, pi_ref, dens_of, acc, ready=None):
    acc[...] = jnp.zeros_like(acc)
    for n, (a, row, col, live, tiles, k) in enumerate(slots(core, idx_refs, tile_refs)):
        if ready is not None:
            ready(n)
        w = (pi_ref[a, row] * (dens_of(row) * live)).astype(BF16)
        acc[col] += jnp.dot(w, tiles[k], preferred_element_type=F32)


def backward(core, idx_refs, tile_refs, v_of, visit, ones=False):
    for a, row, col, live, tiles, k in slots(core, idx_refs, tile_refs):
        v = v_of(col)
        if ones:
            v = jnp.concatenate([v, jnp.ones((HP, B), BF16)], axis=0)
        r = lax.dot_general(v, tiles[k], (((1,), (1,)), ((), ())), preferred_element_type=F32)
        visit(a, row, r * live)


def k_start(density, logits, pay):
    margin = logits[0] - logits[1]
    for n, x in enumerate((coded(density[...] * (1.0 / DENSITY_UNIT)), coded(margin * (1.0 / MARGIN_UNIT)))):
        for b in range(BPZ):
            for c in range(2):
                block = x[c * HP : (c + 1) * HP, b * B : (b + 1) * B]
                for d in range(c, pay.shape[0], 2):
                    pay[d, n, b] = block


def rows_of(scalars):
    return jnp.concatenate([jnp.full((1, B), x, F32) for x in scalars], axis=0)


def arrivals(pay, acc, at):
    for s in range(pay.shape[0]):
        for b in range(ZB):
            put(pay, s, at + b, acc[s * ZB + b].astype(BF16))


def k1(at, own, oth, g, keep, recv, t_own, t_oth, pi, loc, pay, acc):
    c = at[0]
    for d in range(g.shape[0]):
        for b in range(BPZ):
            m = g[d, 1, b].astype(F32) * MARGIN_UNIT
            pi[0, d * BPZ + b] = sigmoid(m)
            pi[1, d * BPZ + b] = sigmoid(-m)
    for n in range(2):
        for b in range(BPZ):
            k, r = keep[n, :, b * B : (b + 1) * B], recv[n, :, b * B : (b + 1) * B]
            loc[n, b] = jnp.where(c == 0, k, r)
            loc[n, BPZ + b] = jnp.where(c == 0, r, k)
    for b in range(ZB):
        put_all(pay, b, loc[0, b].astype(BF16))

    def dens_of(row):
        return g[row // BPZ, 0, row % BPZ].astype(F32) * DENSITY_UNIT

    forward(c, (own, oth), (t_own, t_oth), pi, dens_of, acc)
    arrivals(pay, acc, ZB)


def k2(core, own, oth, g, pi, t_own, t_oth, u1, pay, acc, rows):
    mass = jnp.zeros((HP, 1), F32)
    for b in range(ZB):
        u = get_sum(g, ZB + b)
        u1[b] = u
        mass += jnp.sum(u, axis=1, keepdims=True)
        put_all(pay, 1 + b, u.astype(BF16))
    put_heads(pay, wide_parts(mass))
    acc[...] = jnp.zeros_like(acc)
    rows[...] = jnp.zeros_like(rows)

    def visit(a, row, r):
        acc[row] += pi[a, row] * r[:HP]
        rows[a, row] += r[HP:]

    backward(core[0], (own, oth), (t_own, t_oth), lambda col: g[col // ZB, col % ZB], visit, True)
    for z in range(pay.shape[0]):
        parts = [rows[a, z * ZB + b][0:1] for a in range(A) for b in range(ZB)]
        put(pay, z, 0, jnp.concatenate(parts, axis=0).astype(BF16))
        for b in range(ZB):
            put(pay, z, 1 + ZB + b, acc[z * ZB + b].astype(BF16))


def k3(core, own, oth, g, pi, t_own, t_oth, lv, rsum, pay, acc):
    for b in range(ZB):
        lv[b] = discount * get_sum(g, 1 + ZB + b)
    rsum[...] = get_sum(g, 0)
    put_heads(pay, wide_parts(mass_total(g)))

    def dens_of(row):
        return load(g, row // ZB, 1 + row % ZB).astype(F32)

    forward(core[0], (own, oth), (t_own, t_oth), pi, dens_of, acc)
    arrivals(pay, acc, 0)


def k4(n_states, at, g, pi, u1, rsum, u2, hs, pay):
    m1 = n_states / mass_total(g)
    mass2 = jnp.zeros((HP, 1), F32)
    mass3 = jnp.zeros((HP, 1), F32)
    cols = []
    for b in range(ZB):
        u = get_sum(g, b) * m1
        u2[b] = u
        hs[b : b + 1] = jnp.sum(u1[b] * m1, axis=0, keepdims=True)
        y, k = row_code(u)
        put_all(pay, b, coded(y))
        cols.append(k)
        mass2 += jnp.sum(u, axis=1, keepdims=True)
        row = at[1] * ZB + b
        w0 = (pi[0, row] * u).astype(BF16).astype(F32)
        w1 = (pi[1, row] * u).astype(BF16).astype(F32)
        per = w0 * rsum[b : b + 1] + w1 * rsum[ZB + b : ZB + b + 1]
        mass3 += jnp.sum(per, axis=1, keepdims=True)
    put_heads(pay, pack_cols(cols + mass_cols(mass2) + mass_cols(mass3)))


def k5(core, own, oth, g, pi, t_own, t_oth, pay, acc, dens):
    masses = [jnp.zeros((HP, 1), F32), jnp.zeros((HP, 1), F32)]
    for z in range(g.shape[0]):
        block = g[z, 0].astype(F32)
        for n in range(2):
            masses[n] += mass_of(block, ZB + 3 * n)
        unit = unit_of(block)
        for b in range(ZB):
            dens[z * ZB + b] = load(g, z, b).astype(F32) * col_of(unit, b)
    more = mass_cols(masses[0]) + mass_cols(masses[1])
    forward(core[0], (own, oth), (t_own, t_oth), pi, lambda row: dens[row], acc)
    for s in range(pay.shape[0]):
        put_coded(pay, s, [acc[s * ZB + b] for b in range(ZB)], more)


def k6(n_states, g, u2, hs1, d3, hs):
    mass2 = jnp.zeros((HP, 1), F32)
    mass3 = jnp.zeros((HP, 1), F32)
    for peer in range(g.shape[0]):
        block = g[peer, 0].astype(F32)
        mass2 += mass_of(block, ZB)
        mass3 += mass_of(block, ZB + 3)
    m2, m3 = n_states / mass2, n_states / mass3
    totals = get_coded(g, ZB)
    for b in range(ZB):
        d = totals[b] * m3
        d3[b] = d
        hs[b : b + 1] = hs1[b : b + 1]
        hs[ZB + b : ZB + b + 1] = jnp.sum(u2[b] * m2, axis=0, keepdims=True)
        hs[2 * ZB + b : 2 * ZB + b + 1] = jnp.sum(d, axis=0, keepdims=True)


def k7(at, crowd, hs, hs_oth, loc, lv, rew, pay):
    crowd_rows = rows_of([crowd[at[0] * HP + p] for p in range(HP)])
    mean = (hs[...] + hs_oth[...]) * (1.0 / P_SIZE)
    crowding = jnp.log1p(mean)
    for n in range(3):
        for b in range(ZB):
            r = loc[1, b] - crowd_rows * crowding[n * ZB + b : n * ZB + b + 1]
            if n < 2:
                rew[n, b] = r
            else:
                put_all(pay, b, (r + lv[b]).astype(BF16))


def k8(core, own, oth, g, d3, pi, t_own, t_oth, pay, acc):
    acc[...] = jnp.zeros_like(acc)

    def visit(a, row, r):
        acc[row] += pi[a, row] * r

    backward(core[0], (own, oth), (t_own, t_oth), lambda col: g[col // ZB, col % ZB], visit)
    cols = []
    for b in range(ZB):
        y, k = row_code(d3[b])
        put_all(pay, ZB + b, coded(y))
        cols.append(k)
    for z in range(pay.shape[0]):
        put_coded(pay, z, [acc[z * ZB + b] for b in range(ZB)], cols)


def k9(core, own, oth, g, rew, pi, t_own, t_oth, pay, acc, dens):
    totals = get_coded(g, ZB)
    cols = []
    for b in range(ZB):
        v = rew[1, b] + discount * totals[b]
        y, k = row_code(v)
        put_all(pay, ZB + b, coded(y))
        cols.append(k)
    for z in range(g.shape[0]):
        unit = unit_of(g[z, 0].astype(F32))
        for b in range(ZB):
            dens[z * ZB + b] = load(g, z, ZB + b).astype(F32) * col_of(unit, ZB + b)
    forward(core[0], (own, oth), (t_own, t_oth), pi, lambda row: dens[row], acc)
    for s in range(pay.shape[0]):
        put_coded(pay, s, [acc[s * ZB + b] for b in range(ZB)], cols)


def k10(core, own, oth, g, pi, t_own, t_oth, u4, pay, acc, vals):
    mass = jnp.zeros((HP, 1), F32)
    totals = get_coded(g, ZB)
    for b in range(ZB):
        u4[b] = totals[b]
        mass += jnp.sum(totals[b], axis=1, keepdims=True)
    for s in range(g.shape[0]):
        unit = unit_of(g[s, 0].astype(F32))
        for b in range(ZB):
            vals[s * ZB + b] = (load(g, s, ZB + b).astype(F32) * col_of(unit, ZB + b)).astype(BF16)
    put_heads(pay, wide_parts(mass))
    acc[...] = jnp.zeros_like(acc)

    def visit(a, row, r):
        acc[row] += pi[a, row] * r

    backward(core[0], (own, oth), (t_own, t_oth), lambda col: vals[col], visit)
    for z in range(pay.shape[0]):
        for b in range(ZB):
            put(pay, z, b, acc[z * ZB + b].astype(BF16))


def k11(g, rew, pay):
    for b in range(ZB):
        v = rew[0, b] + discount * get_sum(g, b)
        put_all(pay, b, v.astype(BF16))
    put_heads(pay, wide_parts(mass_total(g)))


def k12(n_states, core, own, oth, g, u4, t_own, t_oth, dkeep, dsend, pay, acc):
    c = core[0]
    m4 = n_states / mass_total(g)
    for b in range(BPZ):
        x, y = u4[b] * m4, u4[BPZ + b] * m4
        dkeep[b] = jnp.where(c == 0, x, y)
        dsend[b] = jnp.where(c == 0, y, x)
    acc[...] = jnp.zeros_like(acc)

    def visit(a, row, r):
        acc[a, row] += r

    backward(c, (own, oth), (t_own, t_oth), lambda col: load(g, col // ZB, col % ZB), visit)
    for z in range(pay.shape[0]):
        put_coded(pay, z, [acc[a, z * ZB + b] for a in range(A) for b in range(ZB)])


def k13(at, g, keep, send):
    c = at[0]
    totals = get_coded(g, A * ZB)
    for a in range(A):
        for b in range(BPZ):
            x, y = totals[a * ZB + b], totals[a * ZB + BPZ + b]
            keep[a, b] = jnp.where(c == 0, x, y)
            send[a, b] = jnp.where(c == 0, y, x)


def k14(at, crowd, keep, recv, dkeep, drecv, density, logits, base, new_logits, value, final):
    c = at[0]
    mean = jnp.sum(density[...], axis=0, keepdims=True) * (1.0 / P_SIZE)
    crowd_rows = rows_of([crowd[p] for p in range(P_SIZE)])
    bite = jnp.concatenate([crowd_rows] * BPZ, axis=1) * jnp.log1p(mean)
    margin = logits[0] - logits[1]
    pis = (sigmoid(margin), sigmoid(-margin))

    def whole(k, r):
        first = jnp.concatenate([k[b] for b in range(BPZ)], axis=1)
        second = jnp.concatenate([r[b] for b in range(BPZ)], axis=1)
        lo = jnp.where(c == 0, first, second)
        hi = jnp.where(c == 0, second, first)
        return jnp.concatenate([lo, hi], axis=0)

    total = jnp.zeros_like(margin)
    for a in range(A):
        av = base[a] - bite + discount * whole(keep[a], recv[a])
        new_logits[a] = logits[a] + step_size * av
        total += pis[a] * av
    value[...] = total
    final[...] = whole(dkeep, drecv)


def body(density0, logits, value_final, base_reward, crowd, tiles, tile_src, tile_dst, tile_count):
    ns = lax.axis_size("src")
    nd = lax.axis_size("dst")
    nz = nd // 2
    n_states = float(density0.shape[1] * ns * nd)
    swap = [(i, i ^ 1) for i in range(nd)]
    groups = [[2 * z + c for z in range(nz)] for c in range(2)]
    me = lax.axis_index("dst").astype(jnp.int32)
    core1 = jnp.stack([me % 2, me // 2])

    def other(x):
        return lax.ppermute(x, "dst", swap)

    def over_z(x):
        return lax.all_to_all(x, "dst", 0, 0, tiled=True, axis_index_groups=groups)

    def over_src(x):
        return lax.all_to_all(x, "src", 0, 0, tiled=True)

    t_own = tiles.reshape(A * TCAP, B, B)
    (pay1,) = call(k_start, [((nd, 2, BPZ, HP, B), I16)], 0)(density0, logits)
    own = jnp.concatenate([tile_src, tile_dst, tile_count[..., None]], axis=3)
    margin = logits[0] - logits[1]
    mean_base = sigmoid(margin) * base_reward[0] + sigmoid(-margin) * base_reward[1]
    both = jnp.stack([value_final, mean_base])
    send = lax.dynamic_slice(both, (0, (1 - core1[0]) * HP, 0), (2, HP, BPZ * B))
    keep = lax.dynamic_slice(both, (0, core1[0] * HP, 0), (2, HP, BPZ * B))
    oth = other(own)
    recv = other(send)
    t_oth = other(t_own)
    ix = (core1, own, oth)
    tt = (t_own, t_oth)
    fwd = [pltpu.VMEM((ns * ZB, HP, B), F32)]
    bwd = [pltpu.VMEM((nz * ZB, HP, B), F32)]
    dens = [pltpu.VMEM((nz * ZB, HP, B), F32)]
    vals = [pltpu.VMEM((ns * ZB, HP, B), BF16)]
    g1 = lax.all_to_all(pay1, "dst", 0, 0, tiled=True)
    pi, loc, pay2 = call(
        k1,
        [((A, nz * ZB, HP, B), F32), ((2, ZB, HP, B), F32), ((ns, 2 * ZB, HP, B), BF16)],
        3,
        fwd,
    )(*ix, g1, keep, recv, *tt)
    g2 = over_src(pay2)
    rows = [pltpu.VMEM((A, nz * ZB, HP, B), F32)]
    u1, pay3 = call(k2, [((ZB, HP, B), F32), ((nz, 1 + 2 * (1 + 2 * ZB), HP, HW), BF16)], 3, bwd + rows)(*ix, g2, pi, *tt)
    g3 = over_z(pay3)
    lv, rsum, pay4 = call(k3, [((ZB, HP, B), F32), ((HP, B), F32), ((ns, 1 + 2 * ZB, HP, HW), BF16)], 3, fwd)(
        *ix, g3, pi, *tt
    )
    g4 = over_src(pay4)
    u2, hs1, pay5 = call(
        lambda *r: k4(n_states, *r), [((ZB, HP, B), F32), ((ZB, B), F32), ((nz, 1 + 2 * ZB, HP, HW), I16)], 1
    )(core1, g4, pi, u1, rsum)
    g5 = over_z(pay5)
    (pay6,) = call(k5, [((ns, 1 + 2 * ZB, HP, HW), I16)], 3, fwd + dens)(*ix, g5, pi, *tt)
    g6 = over_src(pay6)
    d3, hs = call(lambda *r: k6(n_states, *r), [((ZB, HP, B), F32), ((3 * ZB, B), F32)], 0)(g6, u2, hs1)
    hs_oth = other(hs)
    rew, pay7 = call(k7, [((2, ZB, HP, B), F32), ((ns, ZB, HP, B), BF16)], 2)(core1, crowd, hs, hs_oth, loc, lv)
    g7 = over_src(pay7)
    (pay8,) = call(k8, [((nz, 1 + 4 * ZB, HP, HW), I16)], 3, bwd)(*ix, g7, d3, pi, *tt)
    g8 = over_z(pay8)
    (pay9,) = call(k9, [((ns, 1 + 4 * ZB, HP, HW), I16)], 3, fwd + dens)(*ix, g8, rew, pi, *tt)
    g9 = over_src(pay9)
    u4, pay10 = call(k10, [((ZB, HP, B), F32), ((nz, 1 + 2 * ZB, HP, HW), BF16)], 3, bwd + vals)(*ix, g9, pi, *tt)
    g10 = over_z(pay10)
    (pay11,) = call(k11, [((ns, 1 + 2 * ZB, HP, HW), BF16)], 0)(g10, rew)
    g11 = over_src(pay11)
    dkeep, dsend, pay12 = call(
        lambda *r: k12(n_states, *r),
        [((BPZ, HP, B), F32), ((BPZ, HP, B), F32), ((nz, 1 + 2 * A * ZB, HP, HW), I16)],
        3,
        [pltpu.VMEM((A, nz * ZB, HP, B), F32)],
    )(*ix, g11, u4, *tt)
    drecv = other(dsend)
    g12 = over_z(pay12)
    rkeep, rsend = call(k13, [((A, BPZ, HP, B), F32)] * 2, 1)(core1, g12)
    rrecv = other(rsend)
    new_logits, value, final = call(
        k14,
        [(logits.shape, F32), (density0.shape, F32), (density0.shape, F32)],
        2,
    )(core1, crowd, rkeep, rrecv, dkeep, drecv, density0, logits, base_reward)
    return (new_logits, value, final)


def solution(mesh):
    in_specs = (
        P(None, ("src", "dst")),
        P(None, None, ("src", "dst")),
        P(None, ("src", "dst")),
        P(None, None, ("src", "dst")),
        P(),
        P("src", "dst", None, None, None, None),
        P("src", "dst", None, None),
        P("src", "dst", None, None),
        P("src", "dst", None),
    )
    out_specs = (P(None, None, ("src", "dst")), P(None, ("src", "dst")), P(None, ("src", "dst")))
    return jax.shard_map(body, mesh=mesh, in_specs=in_specs, out_specs=out_specs, check_vma=False)
```

```python
import jax
import jax.numpy as jnp
from jax import lax
from jax.experimental import pallas as pl
from jax.experimental.pallas import tpu as pltpu
from jax.sharding import PartitionSpec as P


P_SIZE = 16
A = 2
B = 256
BPZ = 2
TCAP = 8
H = 4

HP = P_SIZE // 2
ZB = 2 * BPZ

discount = 0.9
step_size = 1.0

F32 = jnp.float32
BF16 = jnp.bfloat16


def sigmoid(v):
    return 1.0 / (1.0 + jnp.exp(-v))


HW = B // 2


def split_parts(x):
    hi = x.astype(BF16)
    lo = (x - hi.astype(F32)).astype(BF16)
    return hi, lo


def wide_parts(col):
    hi, lo = split_parts(jnp.broadcast_to(col, (HP, HW // 2)))
    return jnp.concatenate([hi, lo], axis=1)


def mass_total(ref):
    block = jnp.sum(ref[:, 0].astype(F32), axis=0)
    return block[:, 0:1] + block[:, HW // 2 : HW // 2 + 1]


I16 = jnp.int16
TOP = 32766.0
LOG = 0.6931471805599453 / 128.0
DENSITY_UNIT = 5.0 / TOP
MARGIN_UNIT = 12.0 / TOP


def coded(x):
    return jnp.floor(x + 0.5).astype(jnp.int32).astype(I16)


def unit_of(k):
    return jnp.exp(k * LOG) * (1.0 / TOP)


def row_code(x):
    top = jnp.max(jnp.abs(x), axis=1, keepdims=True)
    k = jnp.ceil(jnp.log(jnp.maximum(top, 1e-37)) * (1.0 / LOG)) + 1.0
    return x * (1.0 / unit_of(k)), k


def pack_cols(cols):
    lane = lax.broadcasted_iota(jnp.int32, (HP, HW), 1) // 8
    block = jnp.zeros((HP, HW), F32)
    for n, col in enumerate(cols):
        block = jnp.where(lane == n, col, block)
    return coded(block)


def col_of(block, n):
    return block[:, 8 * n : 8 * n + 1]


def mass_cols(mass):
    y, k = row_code(mass)
    whole = jnp.floor(y)
    return [k, whole, (y - whole) * TOP]


def mass_of(block, n):
    y = col_of(block, n + 1) + col_of(block, n + 2) * (1.0 / TOP)
    return y * unit_of(col_of(block, n))


def put(ref, peer, b, block):
    if ref.shape[-1] == B:
        ref[peer, b] = block
    else:
        ref[peer, 1 + 2 * b] = block[:, :HW]
        ref[peer, 2 + 2 * b] = block[:, HW:]


def load(ref, peer, b):
    if ref.shape[-1] == B:
        return ref[peer, b]
    return jnp.concatenate([ref[peer, 1 + 2 * b], ref[peer, 2 + 2 * b]], axis=1)


def put_all(ref, b, block):
    for peer in range(ref.shape[0]):
        put(ref, peer, b, block)


def put_heads(ref, block):
    for peer in range(ref.shape[0]):
        ref[peer, 0] = block


def get_sum(ref, b):
    if ref.shape[-1] == B:
        return jnp.sum(ref[:, b].astype(F32), axis=0)
    halves = [jnp.sum(ref[:, 1 + 2 * b + n].astype(F32), axis=0) for n in range(2)]
    return jnp.concatenate(halves, axis=1)


def put_coded(ref, peer, blocks, more=()):
    cols = []
    for b, x in enumerate(blocks):
        y, k = row_code(x)
        put(ref, peer, b, coded(y))
        cols.append(k)
    ref[peer, 0] = pack_cols(cols + list(more))


def get_coded(ref, blocks):
    totals = [jnp.zeros((HP, B), F32) for _ in range(blocks)]
    for peer in range(ref.shape[0]):
        unit = unit_of(ref[peer, 0].astype(F32))
        for b in range(blocks):
            totals[b] += load(ref, peer, b).astype(F32) * col_of(unit, b)
    return totals


def call(kernel, outs, n_smem, scratch=(), n_any=0, limit=12 << 20):
    def run(*args):
        specs = [pl.BlockSpec(memory_space=pltpu.SMEM)] * n_smem
        specs += [pl.BlockSpec(memory_space=pltpu.VMEM)] * (len(args) - n_smem - n_any)
        specs += [pl.BlockSpec(memory_space=pl.ANY)] * n_any
        return pl.pallas_call(
            kernel,
            out_shape=[jax.ShapeDtypeStruct(s, d) for s, d in outs],
            in_specs=specs,
            out_specs=[pl.BlockSpec(memory_space=pltpu.VMEM)] * len(outs),
            scratch_shapes=list(scratch),
            compiler_params=pltpu.CompilerParams(vmem_limit_bytes=limit),
        )(*args)

    return run


def slots(core, idx_refs, tile_refs):
    for which in range(2):
        if tile_refs[which] is None:
            continue
        origin = core if which == 0 else 1 - core
        idx = idx_refs[which]
        for a in range(A):
            count = idx[0, 0, a, 2 * TCAP]
            for k in range(TCAP):
                row = idx[0, 0, a, k]
                dst = idx[0, 0, a, TCAP + k]
                col = (dst // BPZ) * ZB + origin * BPZ + dst % BPZ
                live = (k < count).astype(F32)
                yield a, row, col, live, tile_refs[which], a * TCAP + k


def forward(core, idx_refs, tile_refs, pi_ref, dens_of, acc):
    if all(ref is not None for ref in tile_refs):
        acc[...] = jnp.zeros_like(acc)
    for a, row, col, live, tiles, k in slots(core, idx_refs, tile_refs):
        w = (pi_ref[a, row] * (dens_of(row) * live)).astype(BF16)
        acc[col] += jnp.dot(w, tiles[k], preferred_element_type=F32)


def backward(core, idx_refs, tile_refs, v_of, visit, ones=False):
    for a, row, col, live, tiles, k in slots(core, idx_refs, tile_refs):
        v = v_of(col)
        if ones:
            v = jnp.concatenate([v, jnp.ones((HP, B), BF16)], axis=0)
        r = lax.dot_general(v, tiles[k], (((1,), (1,)), ((), ())), preferred_element_type=F32)
        visit(a, row, r * live)


def k_start(density, logits, pay):
    margin = logits[0] - logits[1]
    for n, x in enumerate((coded(density[...] * (1.0 / DENSITY_UNIT)), coded(margin * (1.0 / MARGIN_UNIT)))):
        for b in range(BPZ):
            for c in range(2):
                block = x[c * HP : (c + 1) * HP, b * B : (b + 1) * B]
                for d in range(c, pay.shape[0], 2):
                    pay[d, n, b] = block


def rows_of(scalars):
    return jnp.concatenate([jnp.full((1, B), x, F32) for x in scalars], axis=0)


def arrivals(pay, acc, at):
    for s in range(pay.shape[0]):
        for b in range(ZB):
            put(pay, s, at + b, acc[s * ZB + b].astype(BF16))


def first_density(g):
    return lambda row: g[row // BPZ, 0, row % BPZ].astype(F32) * DENSITY_UNIT


def k1a(at, own, oth, g, keep, recv, t_oth, pi, loc, acc):
    c = at[0]
    for d in range(g.shape[0]):
        for b in range(BPZ):
            m = g[d, 1, b].astype(F32) * MARGIN_UNIT
            pi[0, d * BPZ + b] = sigmoid(m)
            pi[1, d * BPZ + b] = sigmoid(-m)
    for n in range(2):
        for b in range(BPZ):
            k, r = keep[n, :, b * B : (b + 1) * B], recv[n, :, b * B : (b + 1) * B]
            loc[n, b] = jnp.where(c == 0, k, r)
            loc[n, BPZ + b] = jnp.where(c == 0, r, k)
    acc[...] = jnp.zeros_like(acc)
    forward(c, (own, oth), (None, t_oth), pi, first_density(g), acc)


def k1b(at, own, oth, g, loc, pi, part, t_own, pay, acc):
    acc[...] = part[...]
    forward(at[0], (own, oth), (t_own, None), pi, first_density(g), acc)
    for b in range(ZB):
        put_all(pay, b, loc[0, b].astype(BF16))
    arrivals(pay, acc, ZB)


def k2(core, own, oth, g, pi, t_own, t_oth, u1, pay, acc, rows):
    mass = jnp.zeros((HP, 1), F32)
    for b in range(ZB):
        u = get_sum(g, ZB + b)
        u1[b] = u
        mass += jnp.sum(u, axis=1, keepdims=True)
        put_all(pay, 1 + b, u.astype(BF16))
    put_heads(pay, wide_parts(mass))
    acc[...] = jnp.zeros_like(acc)
    rows[...] = jnp.zeros_like(rows)

    def visit(a, row, r):
        acc[row] += pi[a, row] * r[:HP]
        rows[a, row] += r[HP:]

    backward(core[0], (own, oth), (t_own, t_oth), lambda col: g[col // ZB, col % ZB], visit, True)
    for z in range(pay.shape[0]):
        parts = [rows[a, z * ZB + b][0:1] for a in range(A) for b in range(ZB)]
        put(pay, z, 0, jnp.concatenate(parts, axis=0).astype(BF16))
        for b in range(ZB):
            put(pay, z, 1 + ZB + b, acc[z * ZB + b].astype(BF16))


def k3(core, own, oth, g, pi, t_own, t_oth, lv, rsum, pay, acc):
    for b in range(ZB):
        lv[b] = discount * get_sum(g, 1 + ZB + b)
    rsum[...] = get_sum(g, 0)
    put_heads(pay, wide_parts(mass_total(g)))

    def dens_of(row):
        return load(g, row // ZB, 1 + row % ZB).astype(F32)

    forward(core[0], (own, oth), (t_own, t_oth), pi, dens_of, acc)
    arrivals(pay, acc, 0)


def k4(n_states, at, g, pi, u1, rsum, u2, hs, pay):
    m1 = n_states / mass_total(g)
    mass2 = jnp.zeros((HP, 1), F32)
    mass3 = jnp.zeros((HP, 1), F32)
    cols = []
    for b in range(ZB):
        u = get_sum(g, b) * m1
        u2[b] = u
        hs[b : b + 1] = jnp.sum(u1[b] * m1, axis=0, keepdims=True)
        y, k = row_code(u)
        put_all(pay, b, coded(y))
        cols.append(k)
        mass2 += jnp.sum(u, axis=1, keepdims=True)
        row = at[1] * ZB + b
        w0 = (pi[0, row] * u).astype(BF16).astype(F32)
        w1 = (pi[1, row] * u).astype(BF16).astype(F32)
        per = w0 * rsum[b : b + 1] + w1 * rsum[ZB + b : ZB + b + 1]
        mass3 += jnp.sum(per, axis=1, keepdims=True)
    put_heads(pay, pack_cols(cols + mass_cols(mass2) + mass_cols(mass3)))


def k5(core, own, oth, g, pi, t_own, t_oth, pay, acc, dens):
    masses = [jnp.zeros((HP, 1), F32), jnp.zeros((HP, 1), F32)]
    for z in range(g.shape[0]):
        block = g[z, 0].astype(F32)
        for n in range(2):
            masses[n] += mass_of(block, ZB + 3 * n)
        unit = unit_of(block)
        for b in range(ZB):
            dens[z * ZB + b] = load(g, z, b).astype(F32) * col_of(unit, b)
    more = mass_cols(masses[0]) + mass_cols(masses[1])
    forward(core[0], (own, oth), (t_own, t_oth), pi, lambda row: dens[row], acc)
    for s in range(pay.shape[0]):
        put_coded(pay, s, [acc[s * ZB + b] for b in range(ZB)], more)


def k6(n_states, g, u2, hs1, d3, hs):
    mass2 = jnp.zeros((HP, 1), F32)
    mass3 = jnp.zeros((HP, 1), F32)
    for peer in range(g.shape[0]):
        block = g[peer, 0].astype(F32)
        mass2 += mass_of(block, ZB)
        mass3 += mass_of(block, ZB + 3)
    m2, m3 = n_states / mass2, n_states / mass3
    totals = get_coded(g, ZB)
    for b in range(ZB):
        d = totals[b] * m3
        d3[b] = d
        hs[b : b + 1] = hs1[b : b + 1]
        hs[ZB + b : ZB + b + 1] = jnp.sum(u2[b] * m2, axis=0, keepdims=True)
        hs[2 * ZB + b : 2 * ZB + b + 1] = jnp.sum(d, axis=0, keepdims=True)


def k7(at, crowd, hs, hs_oth, loc, lv, rew, pay):
    crowd_rows = rows_of([crowd[at[0] * HP + p] for p in range(HP)])
    mean = (hs[...] + hs_oth[...]) * (1.0 / P_SIZE)
    crowding = jnp.log1p(mean)
    for n in range(3):
        for b in range(ZB):
            r = loc[1, b] - crowd_rows * crowding[n * ZB + b : n * ZB + b + 1]
            if n < 2:
                rew[n, b] = r
            else:
                put_all(pay, b, (r + lv[b]).astype(BF16))


def k8(core, own, oth, g, d3, pi, t_own, t_oth, pay, acc):
    acc[...] = jnp.zeros_like(acc)

    def visit(a, row, r):
        acc[row] += pi[a, row] * r

    backward(core[0], (own, oth), (t_own, t_oth), lambda col: g[col // ZB, col % ZB], visit)
    cols = []
    for b in range(ZB):
        y, k = row_code(d3[b])
        put_all(pay, ZB + b, coded(y))
        cols.append(k)
    for z in range(pay.shape[0]):
        put_coded(pay, z, [acc[z * ZB + b] for b in range(ZB)], cols)


def k9(core, own, oth, g, rew, pi, t_own, t_oth, pay, acc, dens):
    totals = get_coded(g, ZB)
    cols = []
    for b in range(ZB):
        v = rew[1, b] + discount * totals[b]
        y, k = row_code(v)
        put_all(pay, ZB + b, coded(y))
        cols.append(k)
    for z in range(g.shape[0]):
        unit = unit_of(g[z, 0].astype(F32))
        for b in range(ZB):
            dens[z * ZB + b] = load(g, z, ZB + b).astype(F32) * col_of(unit, ZB + b)
    forward(core[0], (own, oth), (t_own, t_oth), pi, lambda row: dens[row], acc)
    for s in range(pay.shape[0]):
        put_coded(pay, s, [acc[s * ZB + b] for b in range(ZB)], cols)


def k10(core, own, oth, g, pi, t_own, t_oth, u4, pay, acc, vals):
    mass = jnp.zeros((HP, 1), F32)
    totals = get_coded(g, ZB)
    for b in range(ZB):
        u4[b] = totals[b]
        mass += jnp.sum(totals[b], axis=1, keepdims=True)
    for s in range(g.shape[0]):
        unit = unit_of(g[s, 0].astype(F32))
        for b in range(ZB):
            vals[s * ZB + b] = (load(g, s, ZB + b).astype(F32) * col_of(unit, ZB + b)).astype(BF16)
    put_heads(pay, wide_parts(mass))
    acc[...] = jnp.zeros_like(acc)

    def visit(a, row, r):
        acc[row] += pi[a, row] * r

    backward(core[0], (own, oth), (t_own, t_oth), lambda col: vals[col], visit)
    for z in range(pay.shape[0]):
        for b in range(ZB):
            put(pay, z, b, acc[z * ZB + b].astype(BF16))


def k11(g, rew, pay):
    for b in range(ZB):
        v = rew[0, b] + discount * get_sum(g, b)
        put_all(pay, b, v.astype(BF16))
    put_heads(pay, wide_parts(mass_total(g)))


def k12(n_states, core, own, oth, g, u4, t_own, t_oth, d4, pay, acc):
    c = core[0]
    m4 = n_states / mass_total(g)
    for b in range(ZB):
        d4[b] = u4[b] * m4
    acc[...] = jnp.zeros_like(acc)

    def visit(a, row, r):
        acc[a, row] += r

    backward(c, (own, oth), (t_own, t_oth), lambda col: load(g, col // ZB, col % ZB), visit)
    for z in range(pay.shape[0]):
        put_coded(pay, z, [acc[a, z * ZB + b] for a in range(A) for b in range(ZB)])


def k13(at, g, d4, keep, send):
    c = at[0]
    totals = get_coded(g, A * ZB) + [d4[b] for b in range(ZB)]
    for a in range(A + 1):
        for b in range(BPZ):
            x, y = totals[a * ZB + b], totals[a * ZB + BPZ + b]
            keep[a, b] = jnp.where(c == 0, x, y)
            send[a, b] = jnp.where(c == 0, y, x)


def k14(at, crowd, keep, recv, density, logits, base, new_logits, value, final):
    c = at[0]
    mean = jnp.sum(density[...], axis=0, keepdims=True) * (1.0 / P_SIZE)
    crowd_rows = rows_of([crowd[p] for p in range(P_SIZE)])
    bite = jnp.concatenate([crowd_rows] * BPZ, axis=1) * jnp.log1p(mean)
    margin = logits[0] - logits[1]
    pis = (sigmoid(margin), sigmoid(-margin))

    def whole(a):
        k, r = keep[a], recv[a]
        first = jnp.concatenate([k[b] for b in range(BPZ)], axis=1)
        second = jnp.concatenate([r[b] for b in range(BPZ)], axis=1)
        lo = jnp.where(c == 0, first, second)
        hi = jnp.where(c == 0, second, first)
        return jnp.concatenate([lo, hi], axis=0)

    total = jnp.zeros_like(margin)
    for a in range(A):
        av = base[a] - bite + discount * whole(a)
        new_logits[a] = logits[a] + step_size * av
        total += pis[a] * av
    value[...] = total
    final[...] = whole(A)


def body(density0, logits, value_final, base_reward, crowd, tiles, tile_src, tile_dst, tile_count):
    ns = lax.axis_size("src")
    nd = lax.axis_size("dst")
    nz = nd // 2
    n_states = float(density0.shape[1] * ns * nd)
    swap = [(i, i ^ 1) for i in range(nd)]
    groups = [[2 * z + c for z in range(nz)] for c in range(2)]
    me = lax.axis_index("dst").astype(jnp.int32)
    core1 = jnp.stack([me % 2, me // 2])

    def other(x):
        return lax.ppermute(x, "dst", swap)

    def over_z(x):
        return lax.all_to_all(x, "dst", 0, 0, tiled=True, axis_index_groups=groups)

    def over_src(x):
        return lax.all_to_all(x, "src", 0, 0, tiled=True)

    t_own = tiles.reshape(A * TCAP, B, B)
    (pay1,) = call(k_start, [((nd, 2, BPZ, HP, B), I16)], 0)(density0, logits)
    own = jnp.concatenate([tile_src, tile_dst, tile_count[..., None]], axis=3)
    margin = logits[0] - logits[1]
    mean_base = sigmoid(margin) * base_reward[0] + sigmoid(-margin) * base_reward[1]
    both = jnp.stack([value_final, mean_base])
    send = lax.dynamic_slice(both, (0, (1 - core1[0]) * HP, 0), (2, HP, BPZ * B))
    keep = lax.dynamic_slice(both, (0, core1[0] * HP, 0), (2, HP, BPZ * B))
    oth = other(own)
    recv = other(send)
    t_oth = other(t_own)
    ix = (core1, own, oth)
    tt = (t_own, t_oth)
    fwd = [pltpu.VMEM((ns * ZB, HP, B), F32)]
    bwd = [pltpu.VMEM((nz * ZB, HP, B), F32)]
    dens = [pltpu.VMEM((nz * ZB, HP, B), F32)]
    vals = [pltpu.VMEM((ns * ZB, HP, B), BF16)]
    g1 = lax.all_to_all(pay1, "dst", 0, 0, tiled=True)
    pi, loc, part = call(
        k1a, [((A, nz * ZB, HP, B), F32), ((2, ZB, HP, B), F32), ((ns * ZB, HP, B), F32)], 3
    )(*ix, g1, keep, recv, t_oth)
    (pay2,) = call(k1b, [((ns, 2 * ZB, HP, B), BF16)], 3, fwd)(*ix, g1, loc, pi, part, t_own)
    g2 = over_src(pay2)
    rows = [pltpu.VMEM((A, nz * ZB, HP, B), F32)]
    u1, pay3 = call(k2, [((ZB, HP, B), F32), ((nz, 1 + 2 * (1 + 2 * ZB), HP, HW), BF16)], 3, bwd + rows)(*ix, g2, pi, *tt)
    g3 = over_z(pay3)
    lv, rsum, pay4 = call(k3, [((ZB, HP, B), F32), ((HP, B), F32), ((ns, 1 + 2 * ZB, HP, HW), BF16)], 3, fwd)(
        *ix, g3, pi, *tt
    )
    g4 = over_src(pay4)
    u2, hs1, pay5 = call(
        lambda *r: k4(n_states, *r), [((ZB, HP, B), F32), ((ZB, B), F32), ((nz, 1 + 2 * ZB, HP, HW), I16)], 1
    )(core1, g4, pi, u1, rsum)
    g5 = over_z(pay5)
    (pay6,) = call(k5, [((ns, 1 + 2 * ZB, HP, HW), I16)], 3, fwd + dens)(*ix, g5, pi, *tt)
    g6 = over_src(pay6)
    d3, hs = call(lambda *r: k6(n_states, *r), [((ZB, HP, B), F32), ((3 * ZB, B), F32)], 0)(g6, u2, hs1)
    hs_oth = other(hs)
    rew, pay7 = call(k7, [((2, ZB, HP, B), F32), ((ns, ZB, HP, B), BF16)], 2)(core1, crowd, hs, hs_oth, loc, lv)
    g7 = over_src(pay7)
    (pay8,) = call(k8, [((nz, 1 + 4 * ZB, HP, HW), I16)], 3, bwd)(*ix, g7, d3, pi, *tt)
    g8 = over_z(pay8)
    (pay9,) = call(k9, [((ns, 1 + 4 * ZB, HP, HW), I16)], 3, fwd + dens)(*ix, g8, rew, pi, *tt)
    g9 = over_src(pay9)
    u4, pay10 = call(k10, [((ZB, HP, B), F32), ((nz, 1 + 2 * ZB, HP, HW), BF16)], 3, bwd + vals)(*ix, g9, pi, *tt)
    g10 = over_z(pay10)
    (pay11,) = call(k11, [((ns, 1 + 2 * ZB, HP, HW), BF16)], 0)(g10, rew)
    g11 = over_src(pay11)
    d4, pay12 = call(
        lambda *r: k12(n_states, *r),
        [((ZB, HP, B), F32), ((nz, 1 + 2 * A * ZB, HP, HW), I16)],
        3,
        [pltpu.VMEM((A, nz * ZB, HP, B), F32)],
    )(*ix, g11, u4, *tt)
    g12 = over_z(pay12)
    rkeep, rsend = call(k13, [((A + 1, BPZ, HP, B), F32)] * 2, 1)(core1, g12, d4)
    rrecv = other(rsend)
    new_logits, value, final = call(
        k14,
        [(logits.shape, F32), (density0.shape, F32), (density0.shape, F32)],
        2,
    )(core1, crowd, rkeep, rrecv, density0, logits, base_reward)
    return (new_logits, value, final)


def solution(mesh):
    in_specs = (
        P(None, ("src", "dst")),
        P(None, None, ("src", "dst")),
        P(None, ("src", "dst")),
        P(None, None, ("src", "dst")),
        P(),
        P("src", "dst", None, None, None, None),
        P("src", "dst", None, None),
        P("src", "dst", None, None),
        P("src", "dst", None),
    )
    out_specs = (P(None, None, ("src", "dst")), P(None, ("src", "dst")), P(None, ("src", "dst")))
    return jax.shard_map(body, mesh=mesh, in_specs=in_specs, out_specs=out_specs, check_vma=False)
```

```python
import jax
import jax.numpy as jnp
from jax import lax
from jax.experimental import pallas as pl
from jax.experimental.pallas import tpu as pltpu
from jax.sharding import PartitionSpec as P


P_SIZE = 16
A = 2
B = 256
BPZ = 2
TCAP = 8
H = 4

HP = P_SIZE // 2
ZB = 2 * BPZ

discount = 0.9
step_size = 1.0

F32 = jnp.float32
BF16 = jnp.bfloat16


def sigmoid(v):
    return 1.0 / (1.0 + jnp.exp(-v))


HW = B // 2


def split_parts(x):
    hi = x.astype(BF16)
    lo = (x - hi.astype(F32)).astype(BF16)
    return hi, lo


def wide_parts(col):
    hi, lo = split_parts(jnp.broadcast_to(col, (HP, HW // 2)))
    return jnp.concatenate([hi, lo], axis=1)


def mass_total(ref):
    block = jnp.sum(ref[:, 0].astype(F32), axis=0)
    return block[:, 0:1] + block[:, HW // 2 : HW // 2 + 1]


I16 = jnp.int16
TOP = 32766.0
LOG = 0.6931471805599453 / 128.0
DENSITY_UNIT = 5.0 / TOP
MARGIN_UNIT = 12.0 / TOP


def coded(x):
    return jnp.floor(x + 0.5).astype(jnp.int32).astype(I16)


def unit_of(k):
    return jnp.exp(k * LOG) * (1.0 / TOP)


def row_code(x):
    top = jnp.max(jnp.abs(x), axis=1, keepdims=True)
    k = jnp.ceil(jnp.log(jnp.maximum(top, 1e-37)) * (1.0 / LOG)) + 1.0
    return x * (1.0 / unit_of(k)), k


def pack_cols(cols):
    lane = lax.broadcasted_iota(jnp.int32, (HP, HW), 1) // 8
    block = jnp.zeros((HP, HW), F32)
    for n, col in enumerate(cols):
        block = jnp.where(lane == n, col, block)
    return coded(block)


def col_of(block, n):
    return block[:, 8 * n : 8 * n + 1]


def mass_cols(mass):
    y, k = row_code(mass)
    whole = jnp.floor(y)
    return [k, whole, (y - whole) * TOP]


def mass_of(block, n):
    y = col_of(block, n + 1) + col_of(block, n + 2) * (1.0 / TOP)
    return y * unit_of(col_of(block, n))


def put(ref, peer, b, block):
    if ref.shape[-1] == B:
        ref[peer, b] = block
    else:
        ref[peer, 1 + 2 * b] = block[:, :HW]
        ref[peer, 2 + 2 * b] = block[:, HW:]


def load(ref, peer, b):
    if ref.shape[-1] == B:
        return ref[peer, b]
    return jnp.concatenate([ref[peer, 1 + 2 * b], ref[peer, 2 + 2 * b]], axis=1)


def put_all(ref, b, block):
    for peer in range(ref.shape[0]):
        put(ref, peer, b, block)


def put_heads(ref, block):
    for peer in range(ref.shape[0]):
        ref[peer, 0] = block


def get_sum(ref, b):
    if ref.shape[-1] == B:
        return jnp.sum(ref[:, b].astype(F32), axis=0)
    halves = [jnp.sum(ref[:, 1 + 2 * b + n].astype(F32), axis=0) for n in range(2)]
    return jnp.concatenate(halves, axis=1)


def put_coded(ref, peer, blocks, more=()):
    cols = []
    for b, x in enumerate(blocks):
        y, k = row_code(x)
        put(ref, peer, b, coded(y))
        cols.append(k)
    ref[peer, 0] = pack_cols(cols + list(more))


def get_coded(ref, blocks):
    totals = [jnp.zeros((HP, B), F32) for _ in range(blocks)]
    for peer in range(ref.shape[0]):
        unit = unit_of(ref[peer, 0].astype(F32))
        for b in range(blocks):
            totals[b] += load(ref, peer, b).astype(F32) * col_of(unit, b)
    return totals


def call(kernel, outs, n_smem, scratch=(), n_any=0, limit=12 << 20):
    def run(*args):
        specs = [pl.BlockSpec(memory_space=pltpu.SMEM)] * n_smem
        specs += [pl.BlockSpec(memory_space=pltpu.VMEM)] * (len(args) - n_smem - n_any)
        specs += [pl.BlockSpec(memory_space=pl.ANY)] * n_any
        return pl.pallas_call(
            kernel,
            out_shape=[jax.ShapeDtypeStruct(s, d) for s, d in outs],
            in_specs=specs,
            out_specs=[pl.BlockSpec(memory_space=pltpu.VMEM)] * len(outs),
            scratch_shapes=list(scratch),
            compiler_params=pltpu.CompilerParams(vmem_limit_bytes=limit),
        )(*args)

    return run


def slots(core, idx_refs, tile_refs):
    for which in range(2):
        if tile_refs[which] is None:
            continue
        origin = core if which == 0 else 1 - core
        idx = idx_refs[which]
        for a in range(A):
            count = idx[0, 0, a, 2 * TCAP]
            for k in range(TCAP):
                row = idx[0, 0, a, k]
                dst = idx[0, 0, a, TCAP + k]
                col = (dst // BPZ) * ZB + origin * BPZ + dst % BPZ
                live = (k < count).astype(F32)
                yield a, row, col, live, tile_refs[which], a * TCAP + k


def forward(core, idx_refs, tile_refs, pi_ref, dens_of, acc):
    if all(ref is not None for ref in tile_refs):
        acc[...] = jnp.zeros_like(acc)
    for a, row, col, live, tiles, k in slots(core, idx_refs, tile_refs):
        w = (pi_ref[a, row] * (dens_of(row) * live)).astype(BF16)
        acc[col] += jnp.dot(w, tiles[k], preferred_element_type=F32)


def backward(core, idx_refs, tile_refs, v_of, visit, ones=False):
    for a, row, col, live, tiles, k in slots(core, idx_refs, tile_refs):
        v = v_of(col)
        if ones:
            v = jnp.concatenate([v, jnp.ones((HP, B), BF16)], axis=0)
        r = lax.dot_general(v, tiles[k], (((1,), (1,)), ((), ())), preferred_element_type=F32)
        visit(a, row, r * live)


def k_start(density, logits, pay):
    margin = logits[0] - logits[1]
    for n, x in enumerate((coded(density[...] * (1.0 / DENSITY_UNIT)), coded(margin * (1.0 / MARGIN_UNIT)))):
        for b in range(BPZ):
            for c in range(2):
                block = x[c * HP : (c + 1) * HP, b * B : (b + 1) * B]
                for d in range(c, pay.shape[0], 2):
                    pay[d, n, b] = block


def rows_of(scalars):
    return jnp.concatenate([jnp.full((1, B), x, F32) for x in scalars], axis=0)


def arrivals(pay, acc, at):
    for s in range(pay.shape[0]):
        for b in range(ZB):
            put(pay, s, at + b, acc[s * ZB + b].astype(BF16))


def first_density(g):
    return lambda row: g[row // BPZ, 0, row % BPZ].astype(F32) * DENSITY_UNIT


def k1a(at, own, oth, g, keep, recv, t_oth, pi, loc, acc):
    c = at[0]
    for d in range(g.shape[0]):
        for b in range(BPZ):
            m = g[d, 1, b].astype(F32) * MARGIN_UNIT
            pi[0, d * BPZ + b] = sigmoid(m)
            pi[1, d * BPZ + b] = sigmoid(-m)
    for n in range(2):
        for b in range(BPZ):
            k, r = keep[n, :, b * B : (b + 1) * B], recv[n, :, b * B : (b + 1) * B]
            loc[n, b] = jnp.where(c == 0, k, r)
            loc[n, BPZ + b] = jnp.where(c == 0, r, k)
    acc[...] = jnp.zeros_like(acc)
    forward(c, (own, oth), (None, t_oth), pi, first_density(g), acc)


def k1b(at, own, oth, g, loc, pi, part, t_own, pay, acc):
    acc[...] = part[...]
    forward(at[0], (own, oth), (t_own, None), pi, first_density(g), acc)
    for b in range(ZB):
        put_all(pay, b, loc[0, b].astype(BF16))
    arrivals(pay, acc, ZB)


def k2(core, own, oth, g, pi, t_own, t_oth, u1, pay, acc, rows):
    mass = jnp.zeros((HP, 1), F32)
    for b in range(ZB):
        u = get_sum(g, ZB + b)
        u1[b] = u
        mass += jnp.sum(u, axis=1, keepdims=True)
        put_all(pay, 1 + b, u.astype(BF16))
    put_heads(pay, wide_parts(mass))
    acc[...] = jnp.zeros_like(acc)
    rows[...] = jnp.zeros_like(rows)

    def visit(a, row, r):
        acc[row] += pi[a, row] * r[:HP]
        rows[a, row] += r[HP:]

    backward(core[0], (own, oth), (t_own, t_oth), lambda col: g[col // ZB, col % ZB], visit, True)
    for z in range(pay.shape[0]):
        parts = [rows[a, z * ZB + b][0:1] for a in range(A) for b in range(ZB)]
        put(pay, z, 0, jnp.concatenate(parts, axis=0).astype(BF16))
        for b in range(ZB):
            put(pay, z, 1 + ZB + b, acc[z * ZB + b].astype(BF16))


def k3(core, own, oth, g, pi, t_own, t_oth, lv, rsum, pay, acc):
    for b in range(ZB):
        lv[b] = discount * get_sum(g, 1 + ZB + b)
    rsum[...] = get_sum(g, 0)
    put_heads(pay, wide_parts(mass_total(g)))

    def dens_of(row):
        return load(g, row // ZB, 1 + row % ZB).astype(F32)

    forward(core[0], (own, oth), (t_own, t_oth), pi, dens_of, acc)
    arrivals(pay, acc, 0)


def k4(n_states, at, g, pi, u1, rsum, u2, hs, pay):
    m1 = n_states / mass_total(g)
    mass2 = jnp.zeros((HP, 1), F32)
    mass3 = jnp.zeros((HP, 1), F32)
    cols = []
    for b in range(ZB):
        u = get_sum(g, b) * m1
        u2[b] = u
        hs[b : b + 1] = jnp.sum(u1[b] * m1, axis=0, keepdims=True)
        y, k = row_code(u)
        put_all(pay, b, coded(y))
        cols.append(k)
        mass2 += jnp.sum(u, axis=1, keepdims=True)
        row = at[1] * ZB + b
        w0 = (pi[0, row] * u).astype(BF16).astype(F32)
        w1 = (pi[1, row] * u).astype(BF16).astype(F32)
        per = w0 * rsum[b : b + 1] + w1 * rsum[ZB + b : ZB + b + 1]
        mass3 += jnp.sum(per, axis=1, keepdims=True)
    put_heads(pay, pack_cols(cols + mass_cols(mass2) + mass_cols(mass3)))


def k5(core, own, oth, g, pi, t_own, t_oth, pay, acc, dens):
    masses = [jnp.zeros((HP, 1), F32), jnp.zeros((HP, 1), F32)]
    for z in range(g.shape[0]):
        block = g[z, 0].astype(F32)
        for n in range(2):
            masses[n] += mass_of(block, ZB + 3 * n)
        unit = unit_of(block)
        for b in range(ZB):
            dens[z * ZB + b] = load(g, z, b).astype(F32) * col_of(unit, b)
    more = mass_cols(masses[0]) + mass_cols(masses[1])
    forward(core[0], (own, oth), (t_own, t_oth), pi, lambda row: dens[row], acc)
    for s in range(pay.shape[0]):
        put_coded(pay, s, [acc[s * ZB + b] for b in range(ZB)], more)


def k6(n_states, g, u2, hs1, d3, hs):
    mass2 = jnp.zeros((HP, 1), F32)
    mass3 = jnp.zeros((HP, 1), F32)
    for peer in range(g.shape[0]):
        block = g[peer, 0].astype(F32)
        mass2 += mass_of(block, ZB)
        mass3 += mass_of(block, ZB + 3)
    m2, m3 = n_states / mass2, n_states / mass3
    totals = get_coded(g, ZB)
    for b in range(ZB):
        d = totals[b] * m3
        d3[b] = d
        hs[b : b + 1] = hs1[b : b + 1]
        hs[ZB + b : ZB + b + 1] = jnp.sum(u2[b] * m2, axis=0, keepdims=True)
        hs[2 * ZB + b : 2 * ZB + b + 1] = jnp.sum(d, axis=0, keepdims=True)


def k7(at, crowd, hs, hs_oth, loc, lv, rew, pay):
    crowd_rows = rows_of([crowd[at[0] * HP + p] for p in range(HP)])
    mean = (hs[...] + hs_oth[...]) * (1.0 / P_SIZE)
    crowding = jnp.log1p(mean)
    for n in range(3):
        for b in range(ZB):
            r = loc[1, b] - crowd_rows * crowding[n * ZB + b : n * ZB + b + 1]
            if n < 2:
                rew[n, b] = r
            else:
                put_all(pay, b, (r + lv[b]).astype(BF16))


def k8(core, own, oth, g, d3, rsum, pi, t_own, t_oth, pay, acc):
    acc[...] = jnp.zeros_like(acc)

    def visit(a, row, r):
        acc[row] += pi[a, row] * r

    backward(core[0], (own, oth), (t_own, t_oth), lambda col: g[col // ZB, col % ZB], visit)
    cols = []
    mass = jnp.zeros((HP, 1), F32)
    for b in range(ZB):
        y, k = row_code(d3[b])
        put_all(pay, ZB + b, coded(y))
        cols.append(k)
        for a in range(A):
            w = (pi[a, core[1] * ZB + b] * d3[b]).astype(BF16).astype(F32)
            mass += jnp.sum(w * rsum[a * ZB + b : a * ZB + b + 1], axis=1, keepdims=True)
    cols += mass_cols(mass)
    for z in range(pay.shape[0]):
        put_coded(pay, z, [acc[z * ZB + b] for b in range(ZB)], cols)


def k9(core, own, oth, g, rew, pi, t_own, t_oth, pay, acc, dens):
    totals = get_coded(g, ZB)
    cols = []
    for b in range(ZB):
        v = rew[1, b] + discount * totals[b]
        y, k = row_code(v)
        put_all(pay, ZB + b, coded(y))
        cols.append(k)
    mass = jnp.zeros((HP, 1), F32)
    for z in range(g.shape[0]):
        block = g[z, 0].astype(F32)
        mass += mass_of(block, 2 * ZB)
        unit = unit_of(block)
        for b in range(ZB):
            dens[z * ZB + b] = load(g, z, ZB + b).astype(F32) * col_of(unit, ZB + b)
    forward(core[0], (own, oth), (t_own, t_oth), pi, lambda row: dens[row], acc)
    for s in range(pay.shape[0]):
        put_coded(pay, s, [acc[s * ZB + b] for b in range(ZB)], cols + mass_cols(mass))


def k10(n_states, core, own, oth, g, pi, t_own, t_oth, d4, pay, acc, vals):
    mass = jnp.zeros((HP, 1), F32)
    totals = get_coded(g, ZB)
    for s in range(g.shape[0]):
        block = g[s, 0].astype(F32)
        mass += mass_of(block, 2 * ZB)
        unit = unit_of(block)
        for b in range(ZB):
            vals[s * ZB + b] = (load(g, s, ZB + b).astype(F32) * col_of(unit, ZB + b)).astype(BF16)
    m4 = n_states / mass
    for b in range(ZB):
        d4[b] = totals[b] * m4
    acc[...] = jnp.zeros_like(acc)

    def visit(a, row, r):
        acc[row] += pi[a, row] * r

    backward(core[0], (own, oth), (t_own, t_oth), lambda col: vals[col], visit)
    for z in range(pay.shape[0]):
        for b in range(ZB):
            put(pay, z, b, acc[z * ZB + b].astype(BF16))


def k11(g, rew, pay):
    for b in range(ZB):
        v = rew[0, b] + discount * get_sum(g, b)
        put_all(pay, b, v.astype(BF16))


def k12(core, own, oth, g, t_own, t_oth, pay, acc):
    c = core[0]
    acc[...] = jnp.zeros_like(acc)

    def visit(a, row, r):
        acc[a, row] += r

    backward(c, (own, oth), (t_own, t_oth), lambda col: load(g, col // ZB, col % ZB), visit)
    for z in range(pay.shape[0]):
        put_coded(pay, z, [acc[a, z * ZB + b] for a in range(A) for b in range(ZB)])


def k13(at, g, d4, keep, send):
    c = at[0]
    totals = get_coded(g, A * ZB) + [d4[b] for b in range(ZB)]
    for a in range(A + 1):
        for b in range(BPZ):
            x, y = totals[a * ZB + b], totals[a * ZB + BPZ + b]
            keep[a, b] = jnp.where(c == 0, x, y)
            send[a, b] = jnp.where(c == 0, y, x)


def k14(at, crowd, keep, recv, density, logits, base, new_logits, value, final):
    c = at[0]
    mean = jnp.sum(density[...], axis=0, keepdims=True) * (1.0 / P_SIZE)
    crowd_rows = rows_of([crowd[p] for p in range(P_SIZE)])
    bite = jnp.concatenate([crowd_rows] * BPZ, axis=1) * jnp.log1p(mean)
    margin = logits[0] - logits[1]
    pis = (sigmoid(margin), sigmoid(-margin))

    def whole(a):
        k, r = keep[a], recv[a]
        first = jnp.concatenate([k[b] for b in range(BPZ)], axis=1)
        second = jnp.concatenate([r[b] for b in range(BPZ)], axis=1)
        lo = jnp.where(c == 0, first, second)
        hi = jnp.where(c == 0, second, first)
        return jnp.concatenate([lo, hi], axis=0)

    total = jnp.zeros_like(margin)
    for a in range(A):
        av = base[a] - bite + discount * whole(a)
        new_logits[a] = logits[a] + step_size * av
        total += pis[a] * av
    value[...] = total
    final[...] = whole(A)


def body(density0, logits, value_final, base_reward, crowd, tiles, tile_src, tile_dst, tile_count):
    ns = lax.axis_size("src")
    nd = lax.axis_size("dst")
    nz = nd // 2
    n_states = float(density0.shape[1] * ns * nd)
    swap = [(i, i ^ 1) for i in range(nd)]
    groups = [[2 * z + c for z in range(nz)] for c in range(2)]
    me = lax.axis_index("dst").astype(jnp.int32)
    core1 = jnp.stack([me % 2, me // 2])

    def other(x):
        return lax.ppermute(x, "dst", swap)

    def over_z(x):
        return lax.all_to_all(x, "dst", 0, 0, tiled=True, axis_index_groups=groups)

    def over_src(x):
        return lax.all_to_all(x, "src", 0, 0, tiled=True)

    t_own = tiles.reshape(A * TCAP, B, B)
    (pay1,) = call(k_start, [((nd, 2, BPZ, HP, B), I16)], 0)(density0, logits)
    own = jnp.concatenate([tile_src, tile_dst, tile_count[..., None]], axis=3)
    margin = logits[0] - logits[1]
    mean_base = sigmoid(margin) * base_reward[0] + sigmoid(-margin) * base_reward[1]
    both = jnp.stack([value_final, mean_base])
    send = lax.dynamic_slice(both, (0, (1 - core1[0]) * HP, 0), (2, HP, BPZ * B))
    keep = lax.dynamic_slice(both, (0, core1[0] * HP, 0), (2, HP, BPZ * B))
    oth = other(own)
    recv = other(send)
    t_oth = other(t_own)
    ix = (core1, own, oth)
    tt = (t_own, t_oth)
    fwd = [pltpu.VMEM((ns * ZB, HP, B), F32)]
    bwd = [pltpu.VMEM((nz * ZB, HP, B), F32)]
    dens = [pltpu.VMEM((nz * ZB, HP, B), F32)]
    vals = [pltpu.VMEM((ns * ZB, HP, B), BF16)]
    g1 = lax.all_to_all(pay1, "dst", 0, 0, tiled=True)
    pi, loc, part = call(
        k1a, [((A, nz * ZB, HP, B), F32), ((2, ZB, HP, B), F32), ((ns * ZB, HP, B), F32)], 3
    )(*ix, g1, keep, recv, t_oth)
    (pay2,) = call(k1b, [((ns, 2 * ZB, HP, B), BF16)], 3, fwd)(*ix, g1, loc, pi, part, t_own)
    g2 = over_src(pay2)
    rows = [pltpu.VMEM((A, nz * ZB, HP, B), F32)]
    u1, pay3 = call(k2, [((ZB, HP, B), F32), ((nz, 1 + 2 * (1 + 2 * ZB), HP, HW), BF16)], 3, bwd + rows)(*ix, g2, pi, *tt)
    g3 = over_z(pay3)
    lv, rsum, pay4 = call(k3, [((ZB, HP, B), F32), ((HP, B), F32), ((ns, 1 + 2 * ZB, HP, HW), BF16)], 3, fwd)(
        *ix, g3, pi, *tt
    )
    g4 = over_src(pay4)
    u2, hs1, pay5 = call(
        lambda *r: k4(n_states, *r), [((ZB, HP, B), F32), ((ZB, B), F32), ((nz, 1 + 2 * ZB, HP, HW), I16)], 1
    )(core1, g4, pi, u1, rsum)
    g5 = over_z(pay5)
    (pay6,) = call(k5, [((ns, 1 + 2 * ZB, HP, HW), I16)], 3, fwd + dens)(*ix, g5, pi, *tt)
    g6 = over_src(pay6)
    d3, hs = call(lambda *r: k6(n_states, *r), [((ZB, HP, B), F32), ((3 * ZB, B), F32)], 0)(g6, u2, hs1)
    hs_oth = other(hs)
    rew, pay7 = call(k7, [((2, ZB, HP, B), F32), ((ns, ZB, HP, B), BF16)], 2)(core1, crowd, hs, hs_oth, loc, lv)
    g7 = over_src(pay7)
    (pay8,) = call(k8, [((nz, 1 + 4 * ZB, HP, HW), I16)], 3, bwd)(*ix, g7, d3, rsum, pi, *tt)
    g8 = over_z(pay8)
    (pay9,) = call(k9, [((ns, 1 + 4 * ZB, HP, HW), I16)], 3, fwd + dens)(*ix, g8, rew, pi, *tt)
    g9 = over_src(pay9)
    d4, pay10 = call(lambda *r: k10(n_states, *r), [((ZB, HP, B), F32), ((nz, ZB, HP, B), BF16)], 3, bwd + vals)(*ix, g9, pi, *tt)
    g10 = over_z(pay10)
    (pay11,) = call(k11, [((ns, ZB, HP, B), BF16)], 0)(g10, rew)
    g11 = over_src(pay11)
    (pay12,) = call(
        k12, [((nz, 1 + 2 * A * ZB, HP, HW), I16)], 3, [pltpu.VMEM((A, nz * ZB, HP, B), F32)]
    )(*ix, g11, *tt)
    g12 = over_z(pay12)
    rkeep, rsend = call(k13, [((A + 1, BPZ, HP, B), F32)] * 2, 1)(core1, g12, d4)
    rrecv = other(rsend)
    new_logits, value, final = call(
        k14,
        [(logits.shape, F32), (density0.shape, F32), (density0.shape, F32)],
        2,
    )(core1, crowd, rkeep, rrecv, density0, logits, base_reward)
    return (new_logits, value, final)


def solution(mesh):
    in_specs = (
        P(None, ("src", "dst")),
        P(None, None, ("src", "dst")),
        P(None, ("src", "dst")),
        P(None, None, ("src", "dst")),
        P(),
        P("src", "dst", None, None, None, None),
        P("src", "dst", None, None),
        P("src", "dst", None, None),
        P("src", "dst", None),
    )
    out_specs = (P(None, None, ("src", "dst")), P(None, ("src", "dst")), P(None, ("src", "dst")))
    return jax.shard_map(body, mesh=mesh, in_specs=in_specs, out_specs=out_specs, check_vma=False)
```
